128 devices in a mesh: tm: 32 (over x, z, core), space: 4 (over y).
Axes of the slice: x: 4, y: 4, z: 4, core: 2. Of those that a mesh axis runs over, the one named last changes fastest.
Arguments:
- state: float32 [64, 3, 128, 1024], P('tm', None, 'space'), may hold values from -2.5 to 2.5
- initial: float32 [3, 128, 1024], P(None, 'space'), may hold values from -2.5 to 2.5
Outputs:
- updated: float32 [64, 3, 128, 1024], P('tm', None, 'space')
The draws below stay inside these ranges and needn't reach their ends.
All inputs are finite; a program needn't handle non-finite values.
Results may differ from the reference program's by a relative error of at most 0.0003.
Values sent between devices are 32-bit elements; how exact they have to be, the bound alone decides.
A program may use at most 128 MiB of HBM per device.

```python
import math
import jax
import jax.numpy as jnp
from jax import lax

NX = 1024
SWEEPS = 4
NT = 64
NY = 128


def shard_levels(own_key, dims, cuts, least, high):
    factor_of = 1.0
    for axis_at, blocks in cuts:
        steps = jax.random.uniform(jax.random.fold_in(jax.random.fold_in(own_key, 6), axis_at), (blocks,), jnp.float32, least / len(cuts), high / len(cuts))
        factor_of = factor_of * jnp.repeat(jnp.exp(steps), dims[axis_at] // blocks).reshape((-1,) + (1,) * (len(dims) - 1 - axis_at))
    return factor_of


def scatter_about(rng, extent, spread, bound, pieces=(), kind=jnp.bfloat16):
    drawn = jax.random.normal(rng, extent, jnp.float32) * spread
    if len(pieces) > 0:
        drawn = shard_levels(rng, extent, pieces, -0.22, 0.18) * drawn
    return jnp.clip(drawn, min=-bound, max=bound).astype(kind)


def setup_inputs(seed: int = 0) -> dict:
    arg_keys = jax.random.split(jax.random.key(seed), 3)
    state = scatter_about(arg_keys[0], (NT, 3, NY, NX), 0.3, 2.5, ((0, 32), (2, 4)), jnp.float32)
    initial = scatter_about(arg_keys[1], (3, NY, NX), 0.3, 2.5, ((1, 4),), jnp.float32)
    return {"state": state, "initial": initial}


circulant_alpha = 0.1
time_step = 0.5
coriolis = 0.3
viscous = 0.2
highest = lax.Precision.HIGHEST


def interior(values):
    return values[..., 1:-1, :]


def column_diff(values):
    return 0.5 * (jnp.roll(values, -1, axis=-1) - jnp.roll(values, 1, axis=-1))[..., 1:-1, :]


def row_diff(values):
    return 0.5 * (values[..., 2:, :] - values[..., :-2, :])


def laplace(values):
    return (values[..., 2:, :] + values[..., :-2, :] + jnp.roll(values, -1, axis=-1)[..., 1:-1, :]
            + jnp.roll(values, 1, axis=-1)[..., 1:-1, :] - 4.0 * values[..., 1:-1, :])


def wrap_rows(values, width):
    return jnp.concatenate([values[..., -width:, :], values, values[..., :width, :]], axis=-2)


def tendency(padded):
    surface = padded[..., 0, :, :]
    eastward = padded[..., 1, :, :]
    northward = padded[..., 2, :, :]
    column_depth = 1.0 + surface
    east_inner = interior(eastward)
    north_inner = interior(northward)
    mass_change = time_step * (column_diff(column_depth * eastward) + row_diff(column_depth * northward)) - viscous * laplace(surface)
    east_change = time_step * (east_inner * column_diff(eastward) + north_inner * row_diff(eastward) + column_diff(surface)) - coriolis * north_inner - viscous * laplace(eastward)
    north_change = time_step * (east_inner * column_diff(northward) + north_inner * row_diff(northward) + row_diff(surface)) + coriolis * east_inner - viscous * laplace(northward)
    return jnp.stack([mass_change, east_change, north_change], axis=-3)


def linear_part(padded):
    surface = padded[..., 0, :, :]
    eastward = padded[..., 1, :, :]
    northward = padded[..., 2, :, :]
    mass_change = time_step * (column_diff(eastward) + row_diff(northward)) - viscous * laplace(surface)
    east_change = time_step * column_diff(surface) - coriolis * interior(northward) - viscous * laplace(eastward)
    north_change = time_step * row_diff(surface) + coriolis * interior(eastward) - viscous * laplace(northward)
    return jnp.stack([mass_change, east_change, north_change], axis=-3)


def pair_apply(factors, values):
    factor = factors[:, :, None, None, None]
    return jnp.stack([factor[0] * values[0] - factor[1] * values[1], factor[2] * values[1] + factor[3] * values[0]])


def sweep_weights():
    return [1.0 / (1.15 - 0.85 * math.cos(math.pi * (2 * sweep + 1) / (2 * SWEEPS))) for sweep in range(SWEEPS)]


def slot_factors(slot_index, total_steps, packed):
    decay_base = circulant_alpha ** (1.0 / total_steps)
    angles = (2.0 * math.pi / total_steps) * slot_index.astype(jnp.float32)
    real_eigen = 1.0 - decay_base * jnp.cos(angles)
    imaginary_eigen = decay_base * jnp.sin(angles)
    real_shift = real_eigen + 4.0 * viscous
    modulus = real_shift * real_shift + imaginary_eigen * imaginary_eigen
    eigen = jnp.stack([real_eigen, imaginary_eigen, real_eigen, imaginary_eigen])
    jacobi = jnp.stack([real_shift / modulus, -imaginary_eigen / modulus, real_shift / modulus, -imaginary_eigen / modulus])
    if packed:
        leading = (slot_index == 0)[None, :]
        zero_part = jnp.zeros_like(real_eigen)
        packed_eigen = jnp.stack([zero_part + (1.0 - decay_base), zero_part, zero_part + (1.0 + decay_base), zero_part])
        packed_jacobi = jnp.stack([zero_part + 1.0 / (1.0 - decay_base + 4.0 * viscous), zero_part,
                                   zero_part + 1.0 / (1.0 + decay_base + 4.0 * viscous), zero_part])
        eigen = jnp.where(leading, packed_eigen, eigen)
        jacobi = jnp.where(leading, packed_jacobi, jacobi)
    return eigen, jacobi


def time_tables(total_steps, packed):
    slot_total = total_steps // 2 if packed else total_steps
    step_ids = jnp.arange(total_steps, dtype=jnp.int32)
    slot_ids = jnp.arange(slot_total, dtype=jnp.int32)
    phase = (slot_ids[:, None] * step_ids[None, :]) % total_steps
    angles = (2.0 * math.pi / total_steps) * phase.astype(jnp.float32)
    decay_base = circulant_alpha ** (1.0 / total_steps)
    growth = decay_base ** step_ids.astype(jnp.float32)
    cosine = jnp.cos(angles)
    sines = jnp.sin(angles)
    forward_real = cosine * growth[None, :]
    forward_imaginary = -sines * growth[None, :]
    inverse_real = cosine
    inverse_imaginary = -sines
    if packed:
        alternate = 1.0 - 2.0 * (step_ids % 2).astype(jnp.float32)
        leading = (slot_ids == 0)[:, None]
        forward_imaginary = jnp.where(leading, (alternate * growth)[None, :], forward_imaginary)
        inverse_real = jnp.where(leading, 1.0, 2.0 * cosine)
        inverse_imaginary = jnp.where(leading, alternate[None, :], -2.0 * sines)
    forward = jnp.concatenate([forward_real, forward_imaginary], axis=0)
    inverse = jnp.concatenate([inverse_real, inverse_imaginary], axis=0).T
    inverse = inverse * (1.0 / (total_steps * growth))[:, None]
    return forward, inverse


def relax(rhs, eigen, jacobi):
    weights = sweep_weights()
    iterate = weights[0] * pair_apply(jacobi, rhs)
    for sweep in range(1, SWEEPS):
        applied = pair_apply(eigen, iterate) + linear_part(wrap_rows(iterate, 1))
        iterate = iterate + weights[sweep] * pair_apply(jacobi, rhs - applied)
    return iterate


def reference(state, initial):
    before = jnp.concatenate([initial[None], state[:-1]], axis=0)

    def one_step(pair):
        current, earlier = pair
        return current - earlier + tendency(wrap_rows(current, 1))

    residual = lax.map(one_step, (state, before))
    forward, inverse = time_tables(NT, False)
    spectrum = jnp.dot(forward, residual.reshape(NT, 3 * NY * NX), precision=highest).reshape(2, NT, 3, NY, NX)
    eigen, jacobi = slot_factors(jnp.arange(NT, dtype=jnp.int32), NT, False)

    def solve_one(item):
        rhs, eigen_one, jacobi_one = item
        return relax(rhs[:, None], eigen_one[:, None], jacobi_one[:, None])[:, 0]

    solution = lax.map(solve_one, (jnp.moveaxis(spectrum, 1, 0), eigen.T, jacobi.T))
    solution = jnp.moveaxis(solution, 0, 1).reshape(2 * NT, 3 * NY * NX)
    correction = jnp.dot(inverse, solution, precision=highest).reshape(NT, 3, NY, NX)
    return state - correction
```

```python
import functools
import math

import jax
import jax.numpy as jnp
from jax import lax
from jax.experimental import pallas as pl
from jax.experimental.pallas import tpu as pltpu
from jax.sharding import PartitionSpec as P

SWEEPS = 4
ALPHA = 0.1
A = 1.0 / 1.8
R = 40
MESH = pl.DeviceIdType.MESH
f32 = jnp.float32


def sweep_weights():
    return [
        1.0 / (1.15 - 0.85 * math.cos(math.pi * (2 * m + 1) / (2 * SWEEPS))) for m in range(SWEEPS)
    ]


def residual_tile(load, j, before):
    sub = lax.broadcasted_iota(jnp.int32, (8, 1), 0)

    def near(f):
        here, after, ahead = load(f, j), load(f, (j + 1) % 5), load(f, (j + 4) % 5)
        cols = here.shape[1]
        north = pltpu.roll(jnp.where(sub == 0, after, here), 7, 0)
        south = pltpu.roll(jnp.where(sub == 7, ahead, here), 1, 0)
        east = pltpu.roll(here, cols - 1, 1)
        west = pltpu.roll(here, 1, 1)
        return here, east, west, north, south

    e, ee, ew, en, es = near(0)
    u, ue, uw, un, us = near(1)
    v, ve, vw, vn, vs = near(2)
    mass = 0.25 * (
        ((1.0 + ee) * ue - (1.0 + ew) * uw) + ((1.0 + en) * vn - (1.0 + es) * vs)
    ) - 0.2 * (ee + ew + en + es - 4.0 * e)
    east = (
        0.25 * (u * (ue - uw) + v * (un - us) + (ee - ew))
        - 0.3 * v
        - 0.2 * (ue + uw + un + us - 4.0 * u)
    )
    north = (
        0.25 * (u * (ve - vw) + v * (vn - vs) + (en - es))
        + 0.3 * u
        - 0.2 * (ve + vw + vn + vs - 4.0 * v)
    )
    return [x - before(f, j) + t for f, (x, t) in enumerate(((e, mass), (u, east), (v, north)))]


def kernel(
    ntm,
    nsp,
    state,
    initial,
    out,
    halo,
    prev,
    prev_halo,
    res,
    send,
    s_buf,
    y_buf,
    corr,
    back,
    ex_send,
    ex_recv,
    in_send,
    in_recv,
    back_send,
    back_recv,
):
    me = lax.axis_index("tm")
    sp = lax.axis_index("space")
    nxt, prv = lax.rem(me + 1, ntm), lax.rem(me + ntm - 1, ntm)
    up, dn = lax.rem(sp + 1, nsp), lax.rem(sp + nsp - 1, nsp)
    cols = state.shape[3]
    steps = 2 * ntm
    width = cols // ntm
    sub8 = lax.broadcasted_iota(jnp.int32, (8, 1), 0)

    barrier = pltpu.get_barrier_semaphore()
    around = [(me, up), (me, dn), (nxt, up), (nxt, dn), (prv, up), (prv, dn)]
    for other in around:
        pl.semaphore_signal(barrier, inc=1, device_id=other, device_id_type=MESH)

    def greet(k, carry):
        pl.semaphore_signal(
            barrier, inc=1, device_id=(lax.rem(me + k, ntm), sp), device_id_type=MESH
        )
        return carry

    lax.fori_loop(1, ntm, greet, 0)
    pl.semaphore_wait(barrier, ntm - 1 + len(around))

    def exchange(i, src, dst, device):
        return pltpu.make_async_remote_copy(
            src_ref=src,
            dst_ref=dst,
            send_sem=ex_send.at[i],
            recv_sem=ex_recv.at[i],
            device_id=device,
            device_id_type=MESH,
        )

    low, high = pl.ds(0, 4), pl.ds(4, 4)
    rows_hi = pl.ds(28, 4)

    def edges():
        return [
            exchange(0, state.at[:, :, low], halo.at[:, :, low], (me, dn)),
            exchange(1, state.at[:, :, rows_hi], halo.at[:, :, high], (me, up)),
        ]

    def handed(last):
        return [
            exchange(2, last, prev, (nxt, sp)),
            exchange(3, last.at[:, low], prev_halo.at[:, low], (nxt, dn)),
            exchange(4, last.at[:, rows_hi], prev_halo.at[:, high], (nxt, up)),
        ]

    normal = edges() + handed(state.at[1])
    for copy in normal[:2]:
        copy.start()

    @pl.when(me != ntm - 1)
    def _():
        for copy in normal[2:]:
            copy.start()

    @pl.when(me == ntm - 1)
    def _():
        for copy in handed(initial):
            copy.start()

    def in_copy(t, p, slot):
        return pltpu.make_async_remote_copy(
            src_ref=send.at[t, p],
            dst_ref=s_buf.at[slot],
            send_sem=in_send.at[t, p],
            recv_sem=in_recv.at[t, lax.div(slot, 2)],
            device_id=(p, sp),
            device_id_type=MESH,
        )

    res[3 * R :, :] = jnp.zeros((res.shape[0] - 3 * R, cols), f32)

    def step_out(t):
        def load(f, j):
            return state[t, f, 8 * j : 8 * j + 8, :] if j < 4 else halo[t, f]

        def before(f, j):
            if t == 1:
                return state[0, f, 8 * j : 8 * j + 8, :] if j < 4 else halo[0, f]
            return prev[f, 8 * j : 8 * j + 8, :] if j < 4 else prev_halo[f]

        last = residual_tile(load, 4, before)
        held = last
        for j in range(4):
            now = residual_tile(load, j, before)
            for f in range(3):
                res[f * R + 8 * j : f * R + 8 * j + 8, :] = pltpu.roll(
                    jnp.where(sub8 < 4, now[f], held[f]), 4, 0
                )
            held = now
        for f in range(3):
            res[f * R + 32 : f * R + 40, :] = pltpu.roll(
                jnp.where(sub8 < 4, last[f], held[f]), 4, 0
            )
        for b in range(cols // 128):
            block = res[:, 128 * b : 128 * b + 128].T
            for i in range(128 // width):
                send[t, b * (128 // width) + i, 0:width, :] = block[width * i : width * i + width]

        def margin(p, carry):
            right, left = lax.rem(p + 1, ntm), lax.rem(p + ntm - 1, ntm)
            send[t, p, width : width + 8, :] = jnp.where(
                sub8 < 4, send[t, right, 0:8, :], send[t, left, width - 8 : width, :]
            )
            return carry

        lax.fori_loop(0, ntm, margin, 0)

        def go(k, carry):
            in_copy(t, lax.rem(me + k, ntm), 2 * me + t).start()
            return carry

        lax.fori_loop(1, ntm, go, 0)
        s_buf[2 * me + t] = send[t, me]

    normal[0].wait_recv()
    normal[1].wait_recv()
    step_out(1)
    for copy in normal[2:]:
        copy.wait_recv()
    step_out(0)

    for copy in normal:
        copy.wait_send()

    def landed(k, carry):
        p = lax.rem(me + k, ntm)
        for t in (1, 0):
            copy = in_copy(t, p, 2 * p + t)
            copy.wait_send()
            copy.wait_recv()
        return carry

    lax.fori_loop(1, ntm, landed, 0)

    lane = lax.broadcasted_iota(jnp.int32, (8, 128), 1)
    field = [(lane >= f * R) & (lane < (f + 1) * R) for f in range(3)]
    lanes = [m.astype(f32) for m in field]
    rows = width + 8

    def wide(x):
        return jnp.concatenate([x] * (rows // 8), axis=0)

    is0 = wide(lanes[0]) > 0.5
    k_col = wide(0.25 * (lanes[0] + lanes[1]))
    k_row = wide(0.25 * (lanes[0] + lanes[2]))
    k_a = wide(0.3 * lanes[1])
    k_b = wide(-0.3 * lanes[2])

    def lhs(s, y):
        a = pltpu.roll(y, 128 - R, 1)
        b = pltpu.roll(y, R, 1)
        a2 = pltpu.roll(y, 128 - 2 * R, 1)
        b2 = pltpu.roll(y, 2 * R, 1)
        scaled = 0.2 * y
        col = k_col * jnp.where(is0, a, b)
        row = k_row * jnp.where(is0, a2, b2)
        right = pltpu.roll(scaled - col, rows - 1, 0)
        left = pltpu.roll(scaled + col, 1, 0)
        north = pltpu.roll(scaled - row, 127, 1)
        south = pltpu.roll(scaled + row, 1, 1)
        return ((s + k_a * a) + (right + left)) + ((north + south) + k_b * b)

    weights = sweep_weights()
    closing = ALPHA / (1.0 - ALPHA * A**steps)
    zero = jnp.zeros((rows, 128), f32)

    def first(n, h):
        h = A * (s_buf[n] + h)
        y_buf[n] = weights[0] * h
        return h

    h = lax.fori_loop(0, steps, first, zero, unroll=4)
    wrap = (A * weights[0] * closing) * h
    for m in range(1, SWEEPS):

        def sweep(n, carry, m=m):
            h, wrap = carry
            y = y_buf[n] + wrap
            h = A * (lhs(s_buf[n], y) + h)
            y_buf[n] = (1.0 - weights[m]) * y + weights[m] * h
            return h, A * wrap

        h, _ = lax.fori_loop(0, steps, sweep, (zero, wrap), unroll=2)
        wrap = (A * weights[m] * closing) * h

    def back_copy(d, slot):
        return pltpu.make_async_remote_copy(
            src_ref=corr.at[d],
            dst_ref=back.at[slot],
            send_sem=back_send.at[d],
            recv_sem=back_recv.at[slot],
            device_id=(d, sp),
            device_id_type=MESH,
        )

    def finish(d, wrap):
        for t in range(2):
            corr[d, t] = pltpu.roll(y_buf[2 * d + t, 0:width, :] + wrap, 124, 1)
            wrap = A * wrap
        return wrap

    lax.fori_loop(0, ntm, finish, wrap[0:width, :])

    def back_go(k, carry):
        back_copy(lax.rem(me + k, ntm), me).start()
        return carry

    lax.fori_loop(1, ntm, back_go, 0)
    back[me] = corr[me]

    def back_landed(k, carry):
        p = lax.rem(me + k, ntm)
        copy = back_copy(p, p)
        copy.wait_send()
        copy.wait_recv()
        return carry

    lax.fori_loop(1, ntm, back_landed, 0)

    for t in range(2):
        for b in range(cols // 128):
            per = 128 // width
            block = jnp.concatenate([back[b * per + i, t] for i in range(per)], axis=0).T
            for f in range(3):
                out[t, f, :, 128 * b : 128 * b + 128] = (
                    state[t, f, :, 128 * b : 128 * b + 128] - block[f * R : f * R + 32, :]
                )


def solution(mesh):
    ntm, nsp = mesh.shape["tm"], mesh.shape["space"]

    def on_device(state, initial):
        cols = state.shape[3]
        width = cols // ntm
        vmem = pltpu.VMEM
        return pl.pallas_call(
            functools.partial(kernel, ntm, nsp),
            out_shape=jax.ShapeDtypeStruct(state.shape, f32),
            in_specs=[pl.BlockSpec(memory_space=vmem)] * 2,
            out_specs=pl.BlockSpec(memory_space=vmem),
            scratch_shapes=[
                vmem((2, 3, 8, cols), f32),
                vmem((3, 32, cols), f32),
                vmem((3, 8, cols), f32),
                vmem((128, cols), f32),
                vmem((2, ntm, width + 8, 128), f32),
                vmem((2 * ntm, width + 8, 128), f32),
                vmem((2 * ntm, width + 8, 128), f32),
                vmem((ntm, 2, width, 128), f32),
                vmem((ntm, 2, width, 128), f32),
                pltpu.SemaphoreType.DMA((5,)),
                pltpu.SemaphoreType.DMA((5,)),
                pltpu.SemaphoreType.DMA((2, ntm)),
                pltpu.SemaphoreType.DMA((2, ntm)),
                pltpu.SemaphoreType.DMA((ntm,)),
                pltpu.SemaphoreType.DMA((ntm,)),
            ],
            compiler_params=pltpu.CompilerParams(
                collective_id=0, has_side_effects=True, vmem_limit_bytes=48 << 20
            ),
        )(state, initial)

    return jax.shard_map(
        on_device,
        mesh=mesh,
        in_specs=(P("tm", None, "space", None), P(None, "space", None)),
        out_specs=P("tm", None, "space", None),
        check_vma=False,
    )
```

```python
import functools
import math

import jax
import jax.numpy as jnp
import numpy as np
from jax import lax
from jax.experimental import pallas as pl
from jax.experimental.pallas import tpu as pltpu
from jax.sharding import PartitionSpec as P

SWEEPS = 4
ALPHA = 0.1
A = 1.0 / 1.8
CHUNK = 8
R = 40
MESH = pl.DeviceIdType.MESH
f32 = jnp.float32


def sweep_weights():
    return [
        1.0 / (1.15 - 0.85 * math.cos(math.pi * (2 * m + 1) / (2 * SWEEPS))) for m in range(SWEEPS)
    ]


def stencil_table():
    table = np.zeros((3, 128, 128), np.float32)
    for f in range(3):
        for r in range(R):
            here = f * R + r
            table[1:, here, here] = 4.0
            for step in (-1, 1):
                if 0 <= r + step < R:
                    table[0, here + step, here] = 4.0
                    if f != 1:
                        table[0, (2 - f) * R + r + step, here] = -5.0 * step
    for r in range(R):
        table[0, 2 * R + r, R + r] = 6.0
        table[0, R + r, 2 * R + r] = -6.0
        table[1, R + r, r] = table[1, r, R + r] = -5.0
        table[2, R + r, r] = table[2, r, R + r] = 5.0
    one = np.concatenate(list(table), axis=1)
    return jnp.asarray(np.concatenate([one, one], axis=0), jnp.bfloat16)


def far_first(shape):
    span = [[(d, min(d, n - d)) for d in range(n)] for n in shape]
    every = [(x, z, c) for x in span[0] for z in span[1] for c in span[2]]
    every.sort(key=lambda d: -(d[0][1] + d[1][1]))
    return [tuple(a[0] for a in d) for d in every if any(a[0] for a in d)]


def residual_tile(load, j, before):
    sub = lax.broadcasted_iota(jnp.int32, (8, 1), 0)

    def near(f):
        here, after, ahead = load(f, j), load(f, (j + 1) % 5), load(f, (j + 4) % 5)
        cols = here.shape[1]
        north = pltpu.roll(jnp.where(sub == 0, after, here), 7, 0)
        south = pltpu.roll(jnp.where(sub == 7, ahead, here), 1, 0)
        east = pltpu.roll(here, cols - 1, 1)
        west = pltpu.roll(here, 1, 1)
        return here, east, west, north, south

    e, ee, ew, en, es = near(0)
    u, ue, uw, un, us = near(1)
    v, ve, vw, vn, vs = near(2)
    mass = 0.25 * (
        ((1.0 + ee) * ue - (1.0 + ew) * uw) + ((1.0 + en) * vn - (1.0 + es) * vs)
    ) - 0.2 * (ee + ew + en + es - 4.0 * e)
    east = (
        0.25 * (u * (ue - uw) + v * (un - us) + (ee - ew))
        - 0.3 * v
        - 0.2 * (ue + uw + un + us - 4.0 * u)
    )
    north = (
        0.25 * (u * (ve - vw) + v * (vn - vs) + (en - es))
        + 0.3 * u
        - 0.2 * (ve + vw + vn + vs - 4.0 * v)
    )
    return [x - before(f, j) + t for f, (x, t) in enumerate(((e, mass), (u, east), (v, north)))]


def kernel(
    ntm,
    nsp,
    state_hbm,
    initial,
    stencil_hbm,
    out,
    state,
    stencil,
    halo,
    prev,
    prev_halo,
    res,
    send,
    s_buf,
    y_buf,
    corr,
    back,
    ex_send,
    ex_recv,
    in_send,
    in_recv,
    back_send,
    back_recv,
    load_sem,
    fade,
):
    me = lax.axis_index("tm")
    sp = lax.axis_index("space")
    nxt, prv = lax.rem(me + 1, ntm), lax.rem(me + ntm - 1, ntm)
    up, dn = lax.rem(sp + 1, nsp), lax.rem(sp + nsp - 1, nsp)
    cols = state.shape[3]
    shape = (4, ntm // 8, 2)
    x, z, c = lax.div(me, 2 * shape[1]), lax.rem(lax.div(me, 2), shape[1]), lax.rem(me, 2)
    others = [
        (lax.rem(x + dx, shape[0]) * shape[1] + lax.rem(z + dz, shape[1])) * 2 + lax.rem(c + dc, 2)
        for dx, dz, dc in far_first(shape)
    ]
    steps = 2 * ntm
    width = cols // ntm
    sub8 = lax.broadcasted_iota(jnp.int32, (8, 1), 0)

    barrier = pltpu.get_barrier_semaphore()
    around = [(me, up), (me, dn), (nxt, up), (nxt, dn), (prv, up), (prv, dn)]
    for other in around:
        pl.semaphore_signal(barrier, inc=1, device_id=other, device_id_type=MESH)

    def greet(k, carry):
        pl.semaphore_signal(
            barrier, inc=1, device_id=(lax.rem(me + k, ntm), sp), device_id_type=MESH
        )
        return carry

    lax.fori_loop(1, ntm, greet, 0)
    loads = [
        pltpu.make_async_copy(state_hbm.at[t], state.at[t], load_sem.at[t]) for t in (1, 0)
    ] + [pltpu.make_async_copy(stencil_hbm, stencil, load_sem.at[2])]
    for copy in loads:
        copy.start()
    pl.semaphore_wait(barrier, ntm - 1 + len(around))

    def exchange(i, src, dst, device):
        return pltpu.make_async_remote_copy(
            src_ref=src,
            dst_ref=dst,
            send_sem=ex_send.at[i],
            recv_sem=ex_recv.at[i],
            device_id=device,
            device_id_type=MESH,
        )

    low, high = pl.ds(0, 4), pl.ds(4, 4)
    rows_hi = pl.ds(28, 4)

    def edges():
        return [
            exchange(0, state_hbm.at[:, :, low], halo.at[:, :, low], (me, dn)),
            exchange(1, state_hbm.at[:, :, rows_hi], halo.at[:, :, high], (me, up)),
        ]

    def handed(last):
        return [
            exchange(2, last, prev, (nxt, sp)),
            exchange(3, last.at[:, low], prev_halo.at[:, low], (nxt, dn)),
            exchange(4, last.at[:, rows_hi], prev_halo.at[:, high], (nxt, up)),
        ]

    normal = edges() + handed(state_hbm.at[1])
    for copy in normal[:2]:
        copy.start()

    @pl.when(me != ntm - 1)
    def _():
        for copy in normal[2:]:
            copy.start()

    @pl.when(me == ntm - 1)
    def _():
        for copy in handed(initial):
            copy.start()

    def in_copy(t, p, slot):
        return pltpu.make_async_remote_copy(
            src_ref=send.at[t, p],
            dst_ref=s_buf.at[slot],
            send_sem=in_send.at[t, p],
            recv_sem=in_recv.at[t, lax.div(slot, 2)],
            device_id=(p, sp),
            device_id_type=MESH,
        )

    res[3 * R :, :] = jnp.zeros((res.shape[0] - 3 * R, cols), f32)

    def step_out(t):
        def load(f, j):
            return state[t, f, 8 * j : 8 * j + 8, :] if j < 4 else halo[t, f]

        def before(f, j):
            if t == 1:
                return state[0, f, 8 * j : 8 * j + 8, :] if j < 4 else halo[0, f]
            return prev[f, 8 * j : 8 * j + 8, :] if j < 4 else prev_halo[f]

        last = residual_tile(load, 4, before)
        held = last
        for j in range(4):
            now = residual_tile(load, j, before)
            for f in range(3):
                res[f * R + 8 * j : f * R + 8 * j + 8, :] = pltpu.roll(
                    jnp.where(sub8 < 4, now[f], held[f]), 4, 0
                )
            held = now
        for f in range(3):
            res[f * R + 32 : f * R + 40, :] = pltpu.roll(
                jnp.where(sub8 < 4, last[f], held[f]), 4, 0
            )
        for b in range(cols // 128):
            block = res[:, 128 * b : 128 * b + 128].T
            for i in range(128 // width):
                send[t, b * (128 // width) + i, 0:width, :] = block[width * i : width * i + width]

        def margin(p, carry):
            right, left = lax.rem(p + 1, ntm), lax.rem(p + ntm - 1, ntm)
            send[t, p, width : width + 8, :] = jnp.where(
                sub8 < 4, send[t, right, 0:8, :], send[t, left, width - 8 : width, :]
            )
            return carry

        lax.fori_loop(0, ntm, margin, 0)

        for p in others:
            in_copy(t, p, 2 * me + t).start()
        s_buf[2 * me + t] = send[t, me]

    gain = jnp.float32(1.0)
    for n in range(ntm):
        fade[n] = gain
        gain = gain * (A * A)
    for copy in loads:
        copy.wait()
    normal[0].wait_recv()
    normal[1].wait_recv()
    step_out(1)
    for copy in normal[2:]:
        copy.wait_recv()
    step_out(0)

    for copy in normal:
        copy.wait_send()

    def landed(k, carry):
        p = lax.rem(me + k, ntm)
        for t in (1, 0):
            copy = in_copy(t, p, 2 * p + t)
            copy.wait_send()
            copy.wait_recv()
        return carry

    lax.fori_loop(1, ntm, landed, 0)

    rows = width + 8
    weights = sweep_weights()
    closing = ALPHA / (1.0 - ALPHA * A**steps)
    zero = jnp.zeros((rows, 128), f32)

    def first(i, h):
        for q in range(CHUNK):
            n = CHUNK * i + q
            h = A * (s_buf[n] + h)
            y_buf[n] = (0.05 * weights[0]) * h
        return h

    h = lax.fori_loop(0, steps // CHUNK, first, zero)
    wrap = (0.05 * A * weights[0] * closing) * h
    for m in range(1, SWEEPS):
        keep, gain = 1.0 - weights[m], 0.05 * weights[m]
        if m == SWEEPS - 1:
            keep, gain = 20.0 * keep, 20.0 * gain

        def sweep(i, carry, keep=keep, gain=gain):
            h, wrap = carry
            ys = []
            for q in range(CHUNK):
                ys.append(y_buf[CHUNK * i + q] + wrap)
                wrap = A * wrap
            y = jnp.concatenate(ys, axis=0)
            high_part = y.astype(jnp.bfloat16)
            low_part = (y - high_part.astype(f32)).astype(jnp.bfloat16)
            parts = jnp.concatenate([high_part, low_part], axis=1)
            mixed = jnp.dot(parts, stencil[...], preferred_element_type=f32)
            for q in range(CHUNK):
                n = CHUNK * i + q
                part = mixed[rows * q : rows * q + rows]
                own, east, west = part[:, :128], part[:, 128:256], part[:, 256:]
                beside = pltpu.roll(east, rows - 1, 0) + pltpu.roll(west, 1, 0)
                h = A * (((s_buf[n] + own) + beside) + h)
                y_buf[n] = keep * ys[q] + gain * h
            return h, wrap

        h, _ = lax.fori_loop(0, steps // CHUNK, sweep, (zero, wrap))
        wrap = (gain * A * closing) * h

    def back_copy(d, slot):
        return pltpu.make_async_remote_copy(
            src_ref=corr.at[d],
            dst_ref=back.at[slot],
            send_sem=back_send.at[d],
            recv_sem=back_recv.at[slot],
            device_id=(d, sp),
            device_id_type=MESH,
        )

    slot_lane = lax.broadcasted_iota(jnp.int32, (width, 128), 1)
    parts = [slot_lane < 32, slot_lane < 64, slot_lane < 96]
    wrap = wrap[0:width, :]

    def finish(d):
        closed = wrap * fade[d]
        one = y_buf[2 * d, 0:width, :] + closed
        two = y_buf[2 * d + 1, 0:width, :] + A * closed
        moved = [pltpu.roll(one, 124 - 8 * f, 1) for f in range(3)]
        corr[d, 0:width, :] = jnp.where(
            parts[0],
            moved[0],
            jnp.where(parts[1], moved[1], jnp.where(parts[2], moved[2], pltpu.roll(two, 92, 1))),
        )
        half = width // 2
        top, end = two[0:half], two[half:width]
        corr[d, width : width + half, :] = jnp.where(
            parts[0][0:half],
            pltpu.roll(top, 84, 1),
            jnp.where(
                parts[1][0:half],
                pltpu.roll(top, 76, 1),
                jnp.where(parts[2][0:half], pltpu.roll(end, 20, 1), pltpu.roll(end, 12, 1)),
            ),
        )

    for i, d in enumerate(others):
        finish(d)
        if i > 0:
            back_copy(others[i - 1], me).start()
    finish(me)
    back_copy(others[-1], me).start()
    back[me] = corr[me]

    def back_landed(k, carry):
        p = lax.rem(me + k, ntm)
        copy = back_copy(p, p)
        copy.wait_send()
        copy.wait_recv()
        return carry

    lax.fori_loop(1, ntm, back_landed, 0)

    per, half = 128 // width, width // 2
    for b in range(cols // 128):
        here = pl.ds(128 * b, 128)
        first_part = jnp.concatenate([back[b * per + i, 0:width] for i in range(per)], axis=0).T
        rest = []
        for i in range(per):
            piece = back[b * per + i, width : width + half]
            rest += [piece, pltpu.roll(piece, 64, 1)]
        second_part = jnp.concatenate(rest, axis=0).T
        for f in range(3):
            out[0, f, :, here] = state[0, f, :, here] - first_part[32 * f : 32 * f + 32]
        out[1, 0, :, here] = state[1, 0, :, here] - first_part[96:128]
        for f in (1, 2):
            out[1, f, :, here] = state[1, f, :, here] - second_part[32 * f - 32 : 32 * f]


def solution(mesh):
    ntm, nsp = mesh.shape["tm"], mesh.shape["space"]

    def on_device(state, initial):
        cols = state.shape[3]
        width = cols // ntm
        vmem = pltpu.VMEM
        return pl.pallas_call(
            functools.partial(kernel, ntm, nsp),
            out_shape=jax.ShapeDtypeStruct(state.shape, f32),
            in_specs=[pl.BlockSpec(memory_space=pl.ANY)] * 3,
            out_specs=pl.BlockSpec(memory_space=vmem),
            scratch_shapes=[
                vmem(state.shape, f32),
                vmem((256, 384), jnp.bfloat16),
                vmem((2, 3, 8, cols), f32),
                vmem((3, 32, cols), f32),
                vmem((3, 8, cols), f32),
                vmem((128, cols), f32),
                vmem((2, ntm, width + 8, 128), f32),
                vmem((2 * ntm, width + 8, 128), f32),
                vmem((2 * ntm, width + 8, 128), f32),
                vmem((ntm, width + width // 2, 128), f32),
                vmem((ntm, width + width // 2, 128), f32),
                pltpu.SemaphoreType.DMA((5,)),
                pltpu.SemaphoreType.DMA((5,)),
                pltpu.SemaphoreType.DMA((2, ntm)),
                pltpu.SemaphoreType.DMA((2, ntm)),
                pltpu.SemaphoreType.DMA((ntm,)),
                pltpu.SemaphoreType.DMA((ntm,)),
                pltpu.SemaphoreType.DMA((3,)),
                pltpu.SMEM((ntm,), f32),
            ],
            compiler_params=pltpu.CompilerParams(
                collective_id=0, has_side_effects=True, vmem_limit_bytes=60 << 20
            ),
        )(state, initial, stencil_table())

    return jax.shard_map(
        on_device,
        mesh=mesh,
        in_specs=(P("tm", None, "space", None), P(None, "space", None)),
        out_specs=P("tm", None, "space", None),
        check_vma=False,
    )
```

```python
import functools
import math

import jax
import jax.numpy as jnp
import numpy as np
from jax import lax
from jax.experimental import pallas as pl
from jax.experimental.pallas import tpu as pltpu
from jax.sharding import PartitionSpec as P

SWEEPS = 4
ALPHA = 0.1
A = 1.0 / 1.8
CHUNK = 32
PARTS = 1
R = 40
MESH = pl.DeviceIdType.MESH
f32 = jnp.float32


def sweep_weights():
    return [
        1.0 / (1.15 - 0.85 * math.cos(math.pi * (2 * m + 1) / (2 * SWEEPS))) for m in range(SWEEPS)
    ]


def stencil_table():
    table = np.zeros((2, 128, 128), np.float32)
    for f in range(3):
        for r in range(R):
            here = f * R + r
            for step in (-1, 1):
                if 0 <= r + step < R:
                    table[0, here + step, here] = 4.0
                    if f != 1:
                        table[0, (2 - f) * R + r + step, here] = -5.0 * step
    for r in range(R):
        table[0, 2 * R + r, R + r] = 6.0
        table[0, R + r, 2 * R + r] = -6.0
        table[1, R + r, r] = table[1, r, R + r] = -5.0
    one = np.concatenate(list(table), axis=1)
    return jnp.asarray(np.concatenate([one, one], axis=0), jnp.bfloat16)


def far_first(shape):
    span = [[(d, min(d, n - d)) for d in range(n)] for n in shape]
    every = [(x, z, c) for x in span[0] for z in span[1] for c in span[2]]
    every.sort(key=lambda d: -(d[0][1] + d[1][1]))
    return [tuple(a[0] for a in d) for d in every if any(a[0] for a in d)]


def residual_tile(load, j, before):
    sub = lax.broadcasted_iota(jnp.int32, (8, 1), 0)

    def near(f):
        here, after, ahead = load(f, j), load(f, (j + 1) % 5), load(f, (j + 4) % 5)
        cols = here.shape[1]
        north = pltpu.roll(jnp.where(sub == 0, after, here), 7, 0)
        south = pltpu.roll(jnp.where(sub == 7, ahead, here), 1, 0)
        east = pltpu.roll(here, cols - 1, 1)
        west = pltpu.roll(here, 1, 1)
        return here, east, west, north, south

    e, ee, ew, en, es = near(0)
    u, ue, uw, un, us = near(1)
    v, ve, vw, vn, vs = near(2)
    mass = 0.25 * (
        ((1.0 + ee) * ue - (1.0 + ew) * uw) + ((1.0 + en) * vn - (1.0 + es) * vs)
    ) - 0.2 * (ee + ew + en + es - 4.0 * e)
    east = (
        0.25 * (u * (ue - uw) + v * (un - us) + (ee - ew))
        - 0.3 * v
        - 0.2 * (ue + uw + un + us - 4.0 * u)
    )
    north = (
        0.25 * (u * (ve - vw) + v * (vn - vs) + (en - es))
        + 0.3 * u
        - 0.2 * (ve + vw + vn + vs - 4.0 * v)
    )
    return [x - before(f, j) + t for f, (x, t) in enumerate(((e, mass), (u, east), (v, north)))]


def kernel(
    ntm,
    nsp,
    state_hbm,
    initial,
    stencil_hbm,
    out,
    state,
    stencil,
    halo,
    prev,
    prev_halo,
    res,
    send,
    s_buf,
    y_buf,
    corr,
    back,
    ex_send,
    ex_recv,
    in_send,
    in_recv,
    back_send,
    back_recv,
    load_sem,
    fade,
):
    me = lax.axis_index("tm")
    sp = lax.axis_index("space")
    nxt, prv = lax.rem(me + 1, ntm), lax.rem(me + ntm - 1, ntm)
    up, dn = lax.rem(sp + 1, nsp), lax.rem(sp + nsp - 1, nsp)
    cols = state.shape[3]
    shape = (4, ntm // 8, 2)
    x, z, c = lax.div(me, 2 * shape[1]), lax.rem(lax.div(me, 2), shape[1]), lax.rem(me, 2)
    others = [
        (lax.rem(x + dx, shape[0]) * shape[1] + lax.rem(z + dz, shape[1])) * 2 + lax.rem(c + dc, 2)
        for dx, dz, dc in far_first(shape)
    ]
    steps = 2 * ntm
    width = cols // ntm
    sub8 = lax.broadcasted_iota(jnp.int32, (8, 1), 0)

    def clear(n, carry):
        s_buf[n, 0:8, :] = jnp.zeros((8, 128), f32)
        s_buf[n, 8 + width : 16 + width, :] = jnp.zeros((8, 128), f32)
        return carry

    lax.fori_loop(0, steps, clear, 0, unroll=8)
    barrier = pltpu.get_barrier_semaphore()
    around = [(me, up), (me, dn), (nxt, up), (nxt, dn), (prv, up), (prv, dn)]
    for other in around:
        pl.semaphore_signal(barrier, inc=1, device_id=other, device_id_type=MESH)

    def greet(k, carry):
        pl.semaphore_signal(
            barrier, inc=1, device_id=(lax.rem(me + k, ntm), sp), device_id_type=MESH
        )
        return carry

    lax.fori_loop(1, ntm, greet, 0)
    loads = [
        pltpu.make_async_copy(state_hbm.at[t], state.at[t], load_sem.at[t]) for t in (1, 0)
    ] + [pltpu.make_async_copy(stencil_hbm, stencil, load_sem.at[2])]
    for copy in loads:
        copy.start()
    pl.semaphore_wait(barrier, ntm - 1 + len(around))

    def exchange(i, src, dst, device):
        return pltpu.make_async_remote_copy(
            src_ref=src,
            dst_ref=dst,
            send_sem=ex_send.at[i],
            recv_sem=ex_recv.at[i],
            device_id=device,
            device_id_type=MESH,
        )

    low, high = pl.ds(0, 4), pl.ds(4, 4)
    rows_hi = pl.ds(28, 4)

    def edges(t):
        return [
            exchange(2 * t, state_hbm.at[t, :, low], halo.at[t, :, low], (me, dn)),
            exchange(2 * t + 1, state_hbm.at[t, :, rows_hi], halo.at[t, :, high], (me, up)),
        ]

    def handed(last):
        return [
            exchange(4, last, prev, (nxt, sp)),
            exchange(5, last.at[:, low], prev_halo.at[:, low], (nxt, dn)),
            exchange(6, last.at[:, rows_hi], prev_halo.at[:, high], (nxt, up)),
        ]

    normal = edges(0) + edges(1) + handed(state_hbm.at[1])
    for copy in normal[:4]:
        copy.start()

    @pl.when(me != ntm - 1)
    def _():
        for copy in normal[4:]:
            copy.start()

    @pl.when(me == ntm - 1)
    def _():
        for copy in handed(initial):
            copy.start()

    own = width // PARTS

    def in_copy(t, i, p, slot):
        start = 5 if i == 0 else 12 + own * i
        end = 11 + width if t == 1 or i == PARTS - 1 else 12 + own * (i + 1)
        rows = pl.ds(start, end - start)
        return pltpu.make_async_remote_copy(
            src_ref=send.at[t, p, rows],
            dst_ref=s_buf.at[slot, rows],
            send_sem=in_send.at[t, i, p],
            recv_sem=in_recv.at[t, i, lax.div(slot, 2)],
            device_id=(p, sp),
            device_id_type=MESH,
        )

    res[3 * R :, :] = jnp.zeros((res.shape[0] - 3 * R, cols), f32)

    def step_out(t):
        def load(f, j):
            return state[t, f, 8 * j : 8 * j + 8, :] if j < 4 else halo[t, f]

        def before(f, j):
            if t == 1:
                return state[0, f, 8 * j : 8 * j + 8, :] if j < 4 else halo[0, f]
            return prev[f, 8 * j : 8 * j + 8, :] if j < 4 else prev_halo[f]

        last = residual_tile(load, 4, before)
        held = last
        for j in range(4):
            now = residual_tile(load, j, before)
            for f in range(3):
                res[f * R + 8 * j : f * R + 8 * j + 8, :] = pltpu.roll(
                    jnp.where(sub8 < 4, now[f], held[f]), 4, 0
                )
            held = now
        for f in range(3):
            res[f * R + 32 : f * R + 40, :] = pltpu.roll(
                jnp.where(sub8 < 4, last[f], held[f]), 4, 0
            )
        for b in range(cols // 128):
            block = res[:, 128 * b : 128 * b + 128].T
            for i in range(128 // width):
                send[t, b * (128 // width) + i, 8 : 8 + width, :] = block[width * i : width * i + width]

        def margin(p, carry):
            right, left = lax.rem(p + 1, ntm), lax.rem(p + ntm - 1, ntm)
            send[t, p, 4:8, :] = send[t, left, 4 + width : 8 + width, :]
            send[t, p, 8 + width : 12 + width, :] = send[t, right, 8:12, :]
            return carry

        lax.fori_loop(0, ntm, margin, 0)

    def go(t, i):
        for p in others:
            in_copy(t, i, p, 2 * me + t).start()

    gain = jnp.float32(1.0)
    for n in range(ntm):
        fade[n] = gain
        gain = gain * (A * A)
    for copy in loads:
        copy.wait()
    for copy in normal[:4]:
        copy.wait_recv()
    step_out(1)
    go(1, 0)
    for copy in normal[4:]:
        copy.wait_recv()
    step_out(0)
    go(0, 0)
    for i in range(1, PARTS):
        for p in others:
            in_copy(0, i - 1, p, 2 * me).wait_send()
            in_copy(0, i, p, 2 * me).start()
    for t in range(2):
        s_buf[2 * me + t] = send[t, me]

    def landed(i):
        def one(k, carry):
            p = lax.rem(me + k, ntm)
            if i == 0:
                in_copy(1, 0, p, 2 * p + 1).wait_recv()
            in_copy(0, i, p, 2 * p).wait_recv()
            return carry

        lax.fori_loop(1, ntm, one, 0)

    rows = own + 8
    weights = sweep_weights()
    closing = ALPHA / (1.0 - ALPHA * A**steps)
    zero = jnp.zeros((rows, 128), f32)

    def solve(i):
        start = 8 + own * i

        def rhs(n):
            after = s_buf[n, start + own : start + own + 8, :]
            ahead = s_buf[n, start - 8 : start, :]
            return jnp.concatenate(
                [s_buf[n, start : start + own, :], jnp.where(sub8 < 4, after, ahead)], axis=0
            )

        def first(k, h):
            for q in range(CHUNK):
                n = CHUNK * k + q
                h = A * (rhs(n) + h)
                y_buf[n] = (0.05 * weights[0]) * h
            return h

        h = lax.fori_loop(0, steps // CHUNK, first, zero)
        wrap = (0.05 * A * weights[0] * closing) * h
        for m in range(1, SWEEPS):
            keep, gain = 1.0 - weights[m], 0.05 * weights[m]
            if m == SWEEPS - 1:
                keep, gain = 20.0 * keep, 20.0 * gain

            def sweep(k, carry, keep=keep, gain=gain):
                h, wrap = carry
                ys = []
                for q in range(CHUNK):
                    ys.append(y_buf[CHUNK * k + q] + wrap)
                    wrap = A * wrap
                y = jnp.concatenate(ys, axis=0)
                high_part = y.astype(jnp.bfloat16)
                low_part = (y - high_part.astype(f32)).astype(jnp.bfloat16)
                both = jnp.concatenate([high_part, low_part], axis=1)
                mixed = jnp.dot(both, stencil[...], preferred_element_type=f32)
                for q in range(CHUNK):
                    n = CHUNK * k + q
                    part = mixed[rows * q : rows * q + rows]
                    here, cross, even = part[:, :128], part[:, 128:], 4.0 * ys[q]
                    beside = pltpu.roll(even + cross, rows - 1, 0) + pltpu.roll(even - cross, 1, 0)
                    h = A * (((rhs(n) + here) + beside) + h)
                    y_buf[n] = keep * ys[q] + gain * h
                return h, wrap

            h, _ = lax.fori_loop(0, steps // CHUNK, sweep, (zero, wrap))
            wrap = (gain * A * closing) * h
        return wrap[0:own, :]

    def back_copy(i, d, slot):
        return pltpu.make_async_remote_copy(
            src_ref=corr.at[d, i],
            dst_ref=back.at[slot, i],
            send_sem=back_send.at[i, d],
            recv_sem=back_recv.at[i, slot],
            device_id=(d, sp),
            device_id_type=MESH,
        )

    lane = lax.broadcasted_iota(jnp.int32, (own, 128), 1)
    below = [lane < 32, lane < 64, lane < 96]
    half = own // 2

    def finish(i, d, wrap):
        closed = wrap * fade[d]
        one = y_buf[2 * d, 0:own, :] + closed
        two = y_buf[2 * d + 1, 0:own, :] + A * closed
        moved = [pltpu.roll(one, 124 - 8 * f, 1) for f in range(3)]
        corr[d, i, 0:own, :] = jnp.where(
            below[0],
            moved[0],
            jnp.where(below[1], moved[1], jnp.where(below[2], moved[2], pltpu.roll(two, 92, 1))),
        )
        top, end = two[0:half], two[half:own]
        corr[d, i, own : own + half, :] = jnp.where(
            below[0][0:half],
            pltpu.roll(top, 84, 1),
            jnp.where(
                below[1][0:half],
                pltpu.roll(top, 76, 1),
                jnp.where(below[2][0:half], pltpu.roll(end, 20, 1), pltpu.roll(end, 12, 1)),
            ),
        )

    for i in range(PARTS):
        landed(i)
        wrap = solve(i)
        for k, d in enumerate(others):
            finish(i, d, wrap)
            if k > 0:
                back_copy(i, others[k - 1], me).start()
        finish(i, me, wrap)
        back_copy(i, others[-1], me).start()
    back[me] = corr[me]

    for copy in normal:
        copy.wait_send()

    def in_sent(k, carry):
        p = lax.rem(me + k, ntm)
        in_copy(1, 0, p, 2 * p + 1).wait_send()
        in_copy(0, PARTS - 1, p, 2 * p).wait_send()
        return carry

    lax.fori_loop(1, ntm, in_sent, 0)

    def back_landed(k, carry):
        p = lax.rem(me + k, ntm)
        for i in range(PARTS):
            copy = back_copy(i, p, p)
            copy.wait_send()
            copy.wait_recv()
        return carry

    lax.fori_loop(1, ntm, back_landed, 0)

    for b in range(cols // 128):
        here = pl.ds(128 * b, 128)
        pieces = [(b * (128 // width) + p, i) for p in range(128 // width) for i in range(PARTS)]
        first_part = jnp.concatenate([back[p, i, 0:own] for p, i in pieces], axis=0).T
        rest = []
        for p, i in pieces:
            piece = back[p, i, own : own + half]
            rest += [piece, pltpu.roll(piece, 64, 1)]
        second_part = jnp.concatenate(rest, axis=0).T
        for f in range(3):
            out[0, f, :, here] = state[0, f, :, here] - first_part[32 * f : 32 * f + 32]
        out[1, 0, :, here] = state[1, 0, :, here] - first_part[96:128]
        for f in (1, 2):
            out[1, f, :, here] = state[1, f, :, here] - second_part[32 * f - 32 : 32 * f]


def solution(mesh):
    ntm, nsp = mesh.shape["tm"], mesh.shape["space"]

    def on_device(state, initial):
        cols = state.shape[3]
        width = cols // ntm
        vmem = pltpu.VMEM
        return pl.pallas_call(
            functools.partial(kernel, ntm, nsp),
            out_shape=jax.ShapeDtypeStruct(state.shape, f32),
            in_specs=[pl.BlockSpec(memory_space=pl.ANY)] * 3,
            out_specs=pl.BlockSpec(memory_space=vmem),
            scratch_shapes=[
                vmem(state.shape, f32),
                vmem((256, 256), jnp.bfloat16),
                vmem((2, 3, 8, cols), f32),
                vmem((3, 32, cols), f32),
                vmem((3, 8, cols), f32),
                vmem((128, cols), f32),
                vmem((2, ntm, width + 16, 128), f32),
                vmem((2 * ntm, width + 16, 128), f32),
                vmem((2 * ntm, width // PARTS + 8, 128), f32),
                vmem((ntm, PARTS, 3 * width // (2 * PARTS), 128), f32),
                vmem((ntm, PARTS, 3 * width // (2 * PARTS), 128), f32),
                pltpu.SemaphoreType.DMA((7,)),
                pltpu.SemaphoreType.DMA((7,)),
                pltpu.SemaphoreType.DMA((2, PARTS, ntm)),
                pltpu.SemaphoreType.DMA((2, PARTS, ntm)),
                pltpu.SemaphoreType.DMA((PARTS, ntm)),
                pltpu.SemaphoreType.DMA((PARTS, ntm)),
                pltpu.SemaphoreType.DMA((3,)),
                pltpu.SMEM((ntm,), f32),
            ],
            compiler_params=pltpu.CompilerParams(
                collective_id=0, has_side_effects=True, vmem_limit_bytes=60 << 20
            ),
        )(state, initial, stencil_table())

    return jax.shard_map(
        on_device,
        mesh=mesh,
        in_specs=(P("tm", None, "space", None), P(None, "space", None)),
        out_specs=P("tm", None, "space", None),
        check_vma=False,
    )
```

```python
import functools
import math

import jax
import jax.numpy as jnp
import numpy as np
from jax import lax
from jax.experimental import pallas as pl
from jax.experimental.pallas import tpu as pltpu
from jax.sharding import PartitionSpec as P

SWEEPS = 4
ALPHA = 0.1
A = 1.0 / 1.8
CHUNK = 32
PARTS = 1
R = 40
MESH = pl.DeviceIdType.MESH
f32 = jnp.float32


def sweep_weights():
    return [
        1.0 / (1.15 - 0.85 * math.cos(math.pi * (2 * m + 1) / (2 * SWEEPS))) for m in range(SWEEPS)
    ]


def stencil_table():
    table = np.zeros((2, 128, 128), np.float32)
    for f in range(3):
        for r in range(R):
            here = f * R + r
            for step in (-1, 1):
                if 0 <= r + step < R:
                    table[0, here + step, here] = 4.0
                    if f != 1:
                        table[0, (2 - f) * R + r + step, here] = -5.0 * step
    for r in range(R):
        table[0, 2 * R + r, R + r] = 6.0
        table[0, R + r, 2 * R + r] = -6.0
        table[1, R + r, r] = table[1, r, R + r] = -5.0
    one = np.concatenate(list(table), axis=1)
    return jnp.asarray(0.25 * np.concatenate([one, one], axis=0), jnp.bfloat16)


def far_first(shape):
    span = [[(d, min(d, n - d)) for d in range(n)] for n in shape]
    every = [(x, z, c) for x in span[0] for z in span[1] for c in span[2]]
    every.sort(key=lambda d: -(d[0][1] + d[1][1]))
    return [tuple(a[0] for a in d) for d in every if any(a[0] for a in d)]


def residual_tile(load, j, before):
    sub = lax.broadcasted_iota(jnp.int32, (8, 1), 0)

    def near(f):
        here, after, ahead = load(f, j), load(f, (j + 1) % 5), load(f, (j + 4) % 5)
        cols = here.shape[1]
        north = pltpu.roll(jnp.where(sub == 0, after, here), 7, 0)
        south = pltpu.roll(jnp.where(sub == 7, ahead, here), 1, 0)
        east = pltpu.roll(here, cols - 1, 1)
        west = pltpu.roll(here, 1, 1)
        return here, east, west, north, south

    e, ee, ew, en, es = near(0)
    u, ue, uw, un, us = near(1)
    v, ve, vw, vn, vs = near(2)
    mass = 0.25 * (
        ((1.0 + ee) * ue - (1.0 + ew) * uw) + ((1.0 + en) * vn - (1.0 + es) * vs)
    ) - 0.2 * (ee + ew + en + es - 4.0 * e)
    east = (
        0.25 * (u * (ue - uw) + v * (un - us) + (ee - ew))
        - 0.3 * v
        - 0.2 * (ue + uw + un + us - 4.0 * u)
    )
    north = (
        0.25 * (u * (ve - vw) + v * (vn - vs) + (en - es))
        + 0.3 * u
        - 0.2 * (ve + vw + vn + vs - 4.0 * v)
    )
    return [x - before(f, j) + t for f, (x, t) in enumerate(((e, mass), (u, east), (v, north)))]


def kernel(
    ntm,
    nsp,
    state_hbm,
    initial,
    stencil_hbm,
    out,
    state,
    stencil,
    halo,
    prev,
    prev_halo,
    res,
    send,
    s_buf,
    y_buf,
    corr,
    back,
    ex_send,
    ex_recv,
    in_send,
    in_recv,
    back_send,
    back_recv,
    load_sem,
    fade,
):
    me = lax.axis_index("tm")
    sp = lax.axis_index("space")
    nxt, prv = lax.rem(me + 1, ntm), lax.rem(me + ntm - 1, ntm)
    up, dn = lax.rem(sp + 1, nsp), lax.rem(sp + nsp - 1, nsp)
    cols = state.shape[3]
    shape = (4, ntm // 8, 2)
    x, z, c = lax.div(me, 2 * shape[1]), lax.rem(lax.div(me, 2), shape[1]), lax.rem(me, 2)
    others = [
        (lax.rem(x + dx, shape[0]) * shape[1] + lax.rem(z + dz, shape[1])) * 2 + lax.rem(c + dc, 2)
        for dx, dz, dc in far_first(shape)
    ]
    steps = 2 * ntm
    width = cols // ntm
    sub8 = lax.broadcasted_iota(jnp.int32, (8, 1), 0)

    def clear(n, carry):
        s_buf[n, 0:8, :] = jnp.zeros((8, 128), f32)
        s_buf[n, 8 + width : 16 + width, :] = jnp.zeros((8, 128), f32)
        return carry

    lax.fori_loop(0, steps, clear, 0, unroll=8)
    barrier = pltpu.get_barrier_semaphore()
    around = [(me, up), (me, dn), (nxt, up), (nxt, dn), (prv, up), (prv, dn)]
    for other in around:
        pl.semaphore_signal(barrier, inc=1, device_id=other, device_id_type=MESH)

    def greet(k, carry):
        pl.semaphore_signal(
            barrier, inc=1, device_id=(lax.rem(me + k, ntm), sp), device_id_type=MESH
        )
        return carry

    lax.fori_loop(1, ntm, greet, 0)
    loads = [
        pltpu.make_async_copy(state_hbm.at[t], state.at[t], load_sem.at[t]) for t in (1, 0)
    ] + [pltpu.make_async_copy(stencil_hbm, stencil, load_sem.at[2])]
    for copy in loads:
        copy.start()
    pl.semaphore_wait(barrier, ntm - 1 + len(around))

    def exchange(i, src, dst, device):
        return pltpu.make_async_remote_copy(
            src_ref=src,
            dst_ref=dst,
            send_sem=ex_send.at[i],
            recv_sem=ex_recv.at[i],
            device_id=device,
            device_id_type=MESH,
        )

    low, high = pl.ds(0, 4), pl.ds(4, 4)
    rows_hi = pl.ds(28, 4)

    def edges(t):
        return [
            exchange(2 * t, state_hbm.at[t, :, low], halo.at[t, :, low], (me, dn)),
            exchange(2 * t + 1, state_hbm.at[t, :, rows_hi], halo.at[t, :, high], (me, up)),
        ]

    def handed(last):
        return [
            exchange(4, last, prev, (nxt, sp)),
            exchange(5, last.at[:, low], prev_halo.at[:, low], (nxt, dn)),
            exchange(6, last.at[:, rows_hi], prev_halo.at[:, high], (nxt, up)),
        ]

    normal = edges(0) + edges(1) + handed(state_hbm.at[1])
    for copy in normal[:4]:
        copy.start()

    @pl.when(me != ntm - 1)
    def _():
        for copy in normal[4:]:
            copy.start()

    @pl.when(me == ntm - 1)
    def _():
        for copy in handed(initial):
            copy.start()

    own = width // PARTS

    def in_copy(t, i, p, slot):
        start = 5 if i == 0 else 12 + own * i
        end = 11 + width if t == 1 or i == PARTS - 1 else 12 + own * (i + 1)
        rows = pl.ds(start, end - start)
        return pltpu.make_async_remote_copy(
            src_ref=send.at[t, p, rows],
            dst_ref=s_buf.at[slot, rows],
            send_sem=in_send.at[t, i, p],
            recv_sem=in_recv.at[t, i, lax.div(slot, 2)],
            device_id=(p, sp),
            device_id_type=MESH,
        )

    res[3 * R :, :] = jnp.zeros((res.shape[0] - 3 * R, cols), f32)

    def step_out(t):
        def load(f, j):
            return state[t, f, 8 * j : 8 * j + 8, :] if j < 4 else halo[t, f]

        def before(f, j):
            if t == 1:
                return state[0, f, 8 * j : 8 * j + 8, :] if j < 4 else halo[0, f]
            return prev[f, 8 * j : 8 * j + 8, :] if j < 4 else prev_halo[f]

        last = residual_tile(load, 4, before)
        held = last
        for j in range(4):
            now = residual_tile(load, j, before)
            for f in range(3):
                res[f * R + 8 * j : f * R + 8 * j + 8, :] = pltpu.roll(
                    jnp.where(sub8 < 4, now[f], held[f]), 4, 0
                )
            held = now
        for f in range(3):
            res[f * R + 32 : f * R + 40, :] = pltpu.roll(
                jnp.where(sub8 < 4, last[f], held[f]), 4, 0
            )
        for b in range(cols // 128):
            block = res[:, 128 * b : 128 * b + 128].T
            for i in range(128 // width):
                send[t, b * (128 // width) + i, 8 : 8 + width, :] = block[width * i : width * i + width]

        def margin(p, carry):
            right, left = lax.rem(p + 1, ntm), lax.rem(p + ntm - 1, ntm)
            send[t, p, 4:8, :] = send[t, left, 4 + width : 8 + width, :]
            send[t, p, 8 + width : 12 + width, :] = send[t, right, 8:12, :]
            return carry

        lax.fori_loop(0, ntm, margin, 0)

    def go(t, i):
        for p in others:
            in_copy(t, i, p, 2 * me + t).start()

    gain = jnp.float32(1.0)
    for n in range(ntm):
        fade[n] = gain
        gain = gain * (A * A)
    for copy in loads:
        copy.wait()
    for copy in normal[:4]:
        copy.wait_recv()
    step_out(1)
    go(1, 0)
    for copy in normal[4:]:
        copy.wait_recv()
    step_out(0)
    go(0, 0)
    for i in range(1, PARTS):
        for p in others:
            in_copy(0, i - 1, p, 2 * me).wait_send()
            in_copy(0, i, p, 2 * me).start()
    for t in range(2):
        s_buf[2 * me + t] = send[t, me]

    def landed(i):
        def one(k, carry):
            p = lax.rem(me + k, ntm)
            if i == 0:
                in_copy(1, 0, p, 2 * p + 1).wait_recv()
            in_copy(0, i, p, 2 * p).wait_recv()
            return carry

        lax.fori_loop(1, ntm, one, 0)

    rows = own + 8
    weights = sweep_weights()
    closing = ALPHA / (1.0 - ALPHA * A**steps)
    zero = jnp.zeros((rows, 128), f32)

    def solve(i):
        start = 8 + own * i

        def rhs(n):
            after = s_buf[n, start + own : start + own + 8, :]
            ahead = s_buf[n, start - 8 : start, :]
            return jnp.concatenate(
                [s_buf[n, start : start + own, :], jnp.where(sub8 < 4, after, ahead)], axis=0
            )

        def first(k, h):
            for q in range(CHUNK):
                n = CHUNK * k + q
                h = A * (rhs(n) + h)
                y_buf[n] = (0.2 * weights[0]) * h
            return h

        h = lax.fori_loop(0, steps // CHUNK, first, zero)
        wrap = (0.2 * A * weights[0] * closing) * h
        for m in range(1, SWEEPS):
            keep, gain = 1.0 - weights[m], 0.2 * weights[m]
            if m == SWEEPS - 1:
                keep, gain = 5.0 * keep, 5.0 * gain

            def sweep(k, carry, keep=keep, gain=gain):
                h, wrap = carry
                ys = []
                for q in range(CHUNK):
                    ys.append(y_buf[CHUNK * k + q] + wrap)
                    wrap = A * wrap
                y = jnp.concatenate(ys, axis=0)
                high_part = y.astype(jnp.bfloat16)
                low_part = (y - high_part.astype(f32)).astype(jnp.bfloat16)
                both = jnp.concatenate([high_part, low_part], axis=1)
                mixed = jnp.dot(both, stencil[...], preferred_element_type=f32)
                for q in range(CHUNK):
                    n = CHUNK * k + q
                    part = mixed[rows * q : rows * q + rows]
                    here, cross, even = part[:, :128], part[:, 128:], ys[q]
                    beside = pltpu.roll(even + cross, rows - 1, 0) + pltpu.roll(even - cross, 1, 0)
                    h = A * (((rhs(n) + here) + beside) + h)
                    y_buf[n] = keep * ys[q] + gain * h
                return h, wrap

            h, _ = lax.fori_loop(0, steps // CHUNK, sweep, (zero, wrap))
            wrap = (gain * A * closing) * h
        return wrap[0:own, :]

    def back_copy(i, d, slot):
        return pltpu.make_async_remote_copy(
            src_ref=corr.at[d, i],
            dst_ref=back.at[slot, i],
            send_sem=back_send.at[i, d],
            recv_sem=back_recv.at[i, slot],
            device_id=(d, sp),
            device_id_type=MESH,
        )

    lane = lax.broadcasted_iota(jnp.int32, (own, 128), 1)
    below = [lane < 32, lane < 64, lane < 96]
    half = own // 2

    def finish(i, d, wrap):
        closed = wrap * fade[d]
        one = y_buf[2 * d, 0:own, :] + closed
        two = y_buf[2 * d + 1, 0:own, :] + A * closed
        moved = [pltpu.roll(one, 124 - 8 * f, 1) for f in range(3)]
        corr[d, i, 0:own, :] = jnp.where(
            below[0],
            moved[0],
            jnp.where(below[1], moved[1], jnp.where(below[2], moved[2], pltpu.roll(two, 92, 1))),
        )
        top, end = two[0:half], two[half:own]
        corr[d, i, own : own + half, :] = jnp.where(
            below[0][0:half],
            pltpu.roll(top, 84, 1),
            jnp.where(
                below[1][0:half],
                pltpu.roll(top, 76, 1),
                jnp.where(below[2][0:half], pltpu.roll(end, 20, 1), pltpu.roll(end, 12, 1)),
            ),
        )

    for i in range(PARTS):
        landed(i)
        wrap = solve(i)
        for k, d in enumerate(others):
            finish(i, d, wrap)
            if k > 0:
                back_copy(i, others[k - 1], me).start()
        finish(i, me, wrap)
        back_copy(i, others[-1], me).start()
    back[me] = corr[me]

    for copy in normal:
        copy.wait_send()

    def in_sent(k, carry):
        p = lax.rem(me + k, ntm)
        in_copy(1, 0, p, 2 * p + 1).wait_send()
        in_copy(0, PARTS - 1, p, 2 * p).wait_send()
        return carry

    lax.fori_loop(1, ntm, in_sent, 0)

    per = 128 // width
    pairs = shape[1] * 2 // per
    pair = lax.div(z * 2, per)
    for dx in sorted(range(shape[0]), key=lambda d: -min(d, shape[0] - d)):
        for dz in range(pairs - 1, -1, -1):
            b = lax.rem(x + dx, shape[0]) * pairs + lax.rem(pair + dz, pairs)
            for k in range(per):
                p = b * per + k
                if dx == 0 and dz == 0:

                    @pl.when(p != me)
                    def _():
                        for i in range(PARTS):
                            back_copy(i, p, p).wait_recv()

                else:
                    for i in range(PARTS):
                        back_copy(i, p, p).wait_recv()
            here = pl.ds(pl.multiple_of(128 * b, 128), 128)
            pieces = [(b * per + k, i) for k in range(per) for i in range(PARTS)]
            first_part = jnp.concatenate([back[p, i, 0:own] for p, i in pieces], axis=0).T
            rest = []
            for p, i in pieces:
                piece = back[p, i, own : own + half]
                rest += [piece, pltpu.roll(piece, 64, 1)]
            second_part = jnp.concatenate(rest, axis=0).T
            for f in range(3):
                out[0, f, :, here] = state[0, f, :, here] - first_part[32 * f : 32 * f + 32]
            out[1, 0, :, here] = state[1, 0, :, here] - first_part[96:128]
            for f in (1, 2):
                out[1, f, :, here] = state[1, f, :, here] - second_part[32 * f - 32 : 32 * f]

    def back_sent(k, carry):
        p = lax.rem(me + k, ntm)
        for i in range(PARTS):
            back_copy(i, p, me).wait_send()
        return carry

    lax.fori_loop(1, ntm, back_sent, 0)


def solution(mesh):
    ntm, nsp = mesh.shape["tm"], mesh.shape["space"]

    def on_device(state, initial):
        cols = state.shape[3]
        width = cols // ntm
        vmem = pltpu.VMEM
        updated = pl.pallas_call(
            functools.partial(kernel, ntm, nsp),
            out_shape=vmem(state.shape, f32),
            in_specs=[pl.BlockSpec(memory_space=pl.ANY)] * 3,
            out_specs=pl.BlockSpec(memory_space=vmem),
            scratch_shapes=[
                vmem(state.shape, f32),
                vmem((256, 256), jnp.bfloat16),
                vmem((2, 3, 8, cols), f32),
                vmem((3, 32, cols), f32),
                vmem((3, 8, cols), f32),
                vmem((128, cols), f32),
                vmem((2, ntm, width + 16, 128), f32),
                vmem((2 * ntm, width + 16, 128), f32),
                vmem((2 * ntm, width // PARTS + 8, 128), f32),
                vmem((ntm, PARTS, 3 * width // (2 * PARTS), 128), f32),
                vmem((ntm, PARTS, 3 * width // (2 * PARTS), 128), f32),
                pltpu.SemaphoreType.DMA((7,)),
                pltpu.SemaphoreType.DMA((7,)),
                pltpu.SemaphoreType.DMA((2, PARTS, ntm)),
                pltpu.SemaphoreType.DMA((2, PARTS, ntm)),
                pltpu.SemaphoreType.DMA((PARTS, ntm)),
                pltpu.SemaphoreType.DMA((PARTS, ntm)),
                pltpu.SemaphoreType.DMA((3,)),
                pltpu.SMEM((ntm,), f32),
            ],
            compiler_params=pltpu.CompilerParams(
                collective_id=0, has_side_effects=True, vmem_limit_bytes=60 << 20
            ),
        )(state, initial, stencil_table())
        return updated

    return jax.shard_map(
        on_device,
        mesh=mesh,
        in_specs=(P("tm", None, "space", None), P(None, "space", None)),
        out_specs=P("tm", None, "space", None),
        check_vma=False,
    )
```

```python
import functools
import math

import jax
import jax.numpy as jnp
import numpy as np
from jax import lax
from jax.experimental import pallas as pl
from jax.experimental.pallas import tpu as pltpu
from jax.sharding import PartitionSpec as P

SWEEPS = 4
ALPHA = 0.1
A = 1.0 / 1.8
CHUNK = 32
PARTS = 1
R = 40
MESH = pl.DeviceIdType.MESH
f32 = jnp.float32


def sweep_weights():
    return [
        1.0 / (1.15 - 0.85 * math.cos(math.pi * (2 * m + 1) / (2 * SWEEPS))) for m in range(SWEEPS)
    ]


def stencil_table():
    table = np.zeros((2, 128, 128), np.float32)
    for f in range(3):
        for r in range(R):
            here = f * R + r
            for step in (-1, 1):
                if 0 <= r + step < R:
                    table[0, here + step, here] = 4.0
                    if f != 1:
                        table[0, (2 - f) * R + r + step, here] = -5.0 * step
    for r in range(R):
        table[0, 2 * R + r, R + r] = 6.0
        table[0, R + r, 2 * R + r] = -6.0
        table[1, R + r, r] = table[1, r, R + r] = -5.0
    one = np.concatenate(list(table), axis=1)
    return jnp.asarray(0.25 * np.concatenate([one, one], axis=0), jnp.bfloat16)


def far_first(shape):
    span = [[(d, min(d, n - d)) for d in range(n)] for n in shape]
    every = [(x, z, c) for x in span[0] for z in span[1] for c in span[2]]
    every.sort(key=lambda d: -(d[0][1] + d[1][1]))
    return [tuple(a[0] for a in d) for d in every if any(a[0] for a in d)]


def residual_tile(load, j, before):
    sub = lax.broadcasted_iota(jnp.int32, (8, 1), 0)

    def near(f):
        here, after, ahead = load(f, j), load(f, (j + 1) % 5), load(f, (j + 4) % 5)
        cols = here.shape[1]
        north = pltpu.roll(jnp.where(sub == 0, after, here), 7, 0)
        south = pltpu.roll(jnp.where(sub == 7, ahead, here), 1, 0)
        east = pltpu.roll(here, cols - 1, 1)
        west = pltpu.roll(here, 1, 1)
        return here, east, west, north, south

    e, ee, ew, en, es = near(0)
    u, ue, uw, un, us = near(1)
    v, ve, vw, vn, vs = near(2)
    mass = 0.25 * (
        ((1.0 + ee) * ue - (1.0 + ew) * uw) + ((1.0 + en) * vn - (1.0 + es) * vs)
    ) - 0.2 * (ee + ew + en + es - 4.0 * e)
    east = (
        0.25 * (u * (ue - uw) + v * (un - us) + (ee - ew))
        - 0.3 * v
        - 0.2 * (ue + uw + un + us - 4.0 * u)
    )
    north = (
        0.25 * (u * (ve - vw) + v * (vn - vs) + (en - es))
        + 0.3 * u
        - 0.2 * (ve + vw + vn + vs - 4.0 * v)
    )
    return [x - before(f, j) + t for f, (x, t) in enumerate(((e, mass), (u, east), (v, north)))]


def kernel(
    ntm,
    nsp,
    state_hbm,
    initial,
    stencil_hbm,
    out,
    state,
    stencil,
    halo,
    prev,
    prev_halo,
    res,
    send,
    s_buf,
    y_buf,
    corr,
    back,
    ex_send,
    ex_recv,
    in_send,
    in_recv,
    back_send,
    back_recv,
    load_sem,
    fade,
):
    me = lax.axis_index("tm")
    sp = lax.axis_index("space")
    nxt, prv = lax.rem(me + 1, ntm), lax.rem(me + ntm - 1, ntm)
    up, dn = lax.rem(sp + 1, nsp), lax.rem(sp + nsp - 1, nsp)
    cols = state.shape[3]
    shape = (4, ntm // 8, 2)
    x, z, c = lax.div(me, 2 * shape[1]), lax.rem(lax.div(me, 2), shape[1]), lax.rem(me, 2)
    others = [
        (lax.rem(x + dx, shape[0]) * shape[1] + lax.rem(z + dz, shape[1])) * 2 + lax.rem(c + dc, 2)
        for dx, dz, dc in far_first(shape)
    ]
    steps = 2 * ntm
    width = cols // ntm
    sub8 = lax.broadcasted_iota(jnp.int32, (8, 1), 0)

    barrier = pltpu.get_barrier_semaphore()
    around = [(me, up), (me, dn), (nxt, up), (nxt, dn), (prv, up), (prv, dn)]
    for other in around:
        pl.semaphore_signal(barrier, inc=1, device_id=other, device_id_type=MESH)

    for p in others:
        pl.semaphore_signal(barrier, inc=1, device_id=(p, sp), device_id_type=MESH)
    loads = [
        pltpu.make_async_copy(state_hbm.at[t], state.at[t], load_sem.at[t]) for t in (1, 0)
    ] + [pltpu.make_async_copy(stencil_hbm, stencil, load_sem.at[2])]
    for copy in loads:
        copy.start()

    def clear(n, carry):
        s_buf[n, 0:5, :] = jnp.zeros((5, 128), f32)
        s_buf[n, 11 + width : 16 + width, :] = jnp.zeros((5, 128), f32)
        return carry

    lax.fori_loop(0, steps, clear, 0, unroll=8)
    pl.semaphore_wait(barrier, ntm - 1 + len(around))

    def exchange(i, src, dst, device):
        return pltpu.make_async_remote_copy(
            src_ref=src,
            dst_ref=dst,
            send_sem=ex_send.at[i],
            recv_sem=ex_recv.at[i],
            device_id=device,
            device_id_type=MESH,
        )

    low, high = pl.ds(0, 4), pl.ds(4, 4)
    rows_hi = pl.ds(28, 4)

    def edges():
        return [
            exchange(0, state_hbm.at[:, :, low], halo.at[:, :, low], (me, dn)),
            exchange(1, state_hbm.at[:, :, rows_hi], halo.at[:, :, high], (me, up)),
        ]

    def handed(last):
        return [
            exchange(4, last, prev, (nxt, sp)),
            exchange(5, last.at[:, low], prev_halo.at[:, low], (nxt, dn)),
            exchange(6, last.at[:, rows_hi], prev_halo.at[:, high], (nxt, up)),
        ]

    normal = edges() + handed(state_hbm.at[1])
    for copy in normal[:2]:
        copy.start()

    @pl.when(me != ntm - 1)
    def _():
        for copy in normal[2:]:
            copy.start()

    @pl.when(me == ntm - 1)
    def _():
        for copy in handed(initial):
            copy.start()

    own = width // PARTS

    def in_copy(t, i, p, slot):
        start = 5 if i == 0 else 12 + own * i
        end = 11 + width if t == 1 or i == PARTS - 1 else 12 + own * (i + 1)
        rows = pl.ds(start, end - start)
        return pltpu.make_async_remote_copy(
            src_ref=send.at[t, p, rows],
            dst_ref=s_buf.at[slot, rows],
            send_sem=in_send.at[t, i, p],
            recv_sem=in_recv.at[t, i, lax.div(slot, 2)],
            device_id=(p, sp),
            device_id_type=MESH,
        )

    res[3 * R :, :] = jnp.zeros((res.shape[0] - 3 * R, cols), f32)

    def step_out(t):
        def load(f, j):
            return state[t, f, 8 * j : 8 * j + 8, :] if j < 4 else halo[t, f]

        def before(f, j):
            if t == 1:
                return state[0, f, 8 * j : 8 * j + 8, :] if j < 4 else halo[0, f]
            return prev[f, 8 * j : 8 * j + 8, :] if j < 4 else prev_halo[f]

        last = residual_tile(load, 4, before)
        held = last
        for j in range(4):
            now = residual_tile(load, j, before)
            for f in range(3):
                res[f * R + 8 * j : f * R + 8 * j + 8, :] = pltpu.roll(
                    jnp.where(sub8 < 4, now[f], held[f]), 4, 0
                )
            held = now
        for f in range(3):
            res[f * R + 32 : f * R + 40, :] = pltpu.roll(
                jnp.where(sub8 < 4, last[f], held[f]), 4, 0
            )
        for b in range(cols // 128):
            block = res[:, 128 * b : 128 * b + 128].T
            for i in range(128 // width):
                p = b * (128 // width) + i
                mine = block[width * i : width * i + width]
                send[t, p, 8 : 8 + width, :] = mine
                send[t, (p + 1) % ntm, 4:8, :] = mine[width - 4 :]
                send[t, (p - 1) % ntm, 8 + width : 12 + width, :] = mine[:4]

    def go(t, i):
        for p in others:
            in_copy(t, i, p, 2 * me + t).start()

    gain = jnp.float32(1.0)
    for n in range(ntm):
        fade[n] = gain
        gain = gain * (A * A)
    for copy in loads:
        copy.wait()
    for copy in normal[:2]:
        copy.wait_recv()
    step_out(1)
    go(1, 0)
    for copy in normal[2:]:
        copy.wait_recv()
    step_out(0)
    go(0, 0)
    for i in range(1, PARTS):
        for p in others:
            in_copy(0, i - 1, p, 2 * me).wait_send()
            in_copy(0, i, p, 2 * me).start()
    for t in range(2):
        s_buf[2 * me + t, 5 : 11 + width, :] = send[t, me, 5 : 11 + width, :]

    def landed(i):
        def one(k, carry):
            p = lax.rem(me + k, ntm)
            if i == 0:
                in_copy(1, 0, p, 2 * p + 1).wait_recv()
            in_copy(0, i, p, 2 * p).wait_recv()
            return carry

        lax.fori_loop(1, ntm, one, 0)

    rows = own + 8
    weights = sweep_weights()
    closing = ALPHA / (1.0 - ALPHA * A**steps)
    zero = jnp.zeros((rows, 128), f32)

    def solve(i):
        start = 8 + own * i

        def rhs(n):
            after = s_buf[n, start + own : start + own + 8, :]
            ahead = s_buf[n, start - 8 : start, :]
            return jnp.concatenate(
                [s_buf[n, start : start + own, :], jnp.where(sub8 < 4, after, ahead)], axis=0
            )

        def first(k, h):
            for q in range(CHUNK):
                n = CHUNK * k + q
                h = A * (rhs(n) + h)
                y_buf[n] = (0.2 * weights[0]) * h
            return h

        h = lax.fori_loop(0, steps // CHUNK, first, zero)
        wrap = (0.2 * A * weights[0] * closing) * h
        for m in range(1, SWEEPS):
            keep, gain = 1.0 - weights[m], 0.2 * weights[m]
            kept = rows
            if m == SWEEPS - 1:
                keep, gain, kept = 5.0 * keep, 5.0 * gain, own

            def sweep(k, carry, keep=keep, gain=gain, kept=kept):
                h, wrap = carry
                ys = []
                for q in range(CHUNK):
                    ys.append(y_buf[CHUNK * k + q] + wrap)
                    wrap = A * wrap
                y = jnp.concatenate(ys, axis=0)
                high_part = y.astype(jnp.bfloat16)
                low_part = (y - high_part.astype(f32)).astype(jnp.bfloat16)
                both = jnp.concatenate([high_part, low_part], axis=1)
                mixed = jnp.dot(both, stencil[...], preferred_element_type=f32)
                for q in range(CHUNK):
                    n = CHUNK * k + q
                    part = mixed[rows * q : rows * q + rows]
                    here, cross, even = part[:, :128], part[:, 128:], ys[q]
                    beside = pltpu.roll(even + cross, rows - 1, 0) + pltpu.roll(even - cross, 1, 0)
                    s = rhs(n) if kept == rows else s_buf[n, start : start + own, :]
                    h = A * (((s + here[:kept]) + beside[:kept]) + h)
                    y_buf[n, 0:kept, :] = keep * ys[q][:kept] + gain * h
                return h, wrap

            h, _ = lax.fori_loop(0, steps // CHUNK, sweep, (zero[:kept], wrap))
            wrap = (gain * A * closing) * h
        return wrap

    def back_copy(i, d, slot):
        return pltpu.make_async_remote_copy(
            src_ref=corr.at[d, i],
            dst_ref=back.at[slot, i],
            send_sem=back_send.at[i, d],
            recv_sem=back_recv.at[i, slot],
            device_id=(d, sp),
            device_id_type=MESH,
        )

    lane = lax.broadcasted_iota(jnp.int32, (own, 128), 1)
    below = [lane < 32, lane < 64, lane < 96]
    half = own // 2

    def finish(i, d, wrap):
        closed = wrap * fade[d]
        one = y_buf[2 * d, 0:own, :] + closed
        two = y_buf[2 * d + 1, 0:own, :] + A * closed
        moved = [pltpu.roll(one, 124 - 8 * f, 1) for f in range(3)]
        corr[d, i, 0:own, :] = jnp.where(
            below[0],
            moved[0],
            jnp.where(below[1], moved[1], jnp.where(below[2], moved[2], pltpu.roll(two, 92, 1))),
        )
        top, end = two[0:half], two[half:own]
        corr[d, i, own : own + half, :] = jnp.where(
            below[0][0:half],
            pltpu.roll(top, 84, 1),
            jnp.where(
                below[1][0:half],
                pltpu.roll(top, 76, 1),
                jnp.where(below[2][0:half], pltpu.roll(end, 20, 1), pltpu.roll(end, 12, 1)),
            ),
        )

    for i in range(PARTS):
        landed(i)
        wrap = solve(i)
        for k, d in enumerate(others):
            finish(i, d, wrap)
            if k > 0:
                back_copy(i, others[k - 1], me).start()
        finish(i, me, wrap)
        back_copy(i, others[-1], me).start()
    back[me] = corr[me]

    for copy in normal:
        copy.wait_send()

    def in_sent(k, carry):
        p = lax.rem(me + k, ntm)
        in_copy(1, 0, p, 2 * p + 1).wait_send()
        in_copy(0, PARTS - 1, p, 2 * p).wait_send()
        return carry

    lax.fori_loop(1, ntm, in_sent, 0)

    per = 128 // width
    pairs = shape[1] * 2 // per
    pair = lax.div(z * 2, per)
    for dx in sorted(range(shape[0]), key=lambda d: -min(d, shape[0] - d)):
        for dz in range(pairs - 1, -1, -1):
            b = lax.rem(x + dx, shape[0]) * pairs + lax.rem(pair + dz, pairs)
            for k in range(per):
                p = b * per + k
                if dx == 0 and dz == 0:

                    @pl.when(p != me)
                    def _():
                        for i in range(PARTS):
                            back_copy(i, p, p).wait_recv()

                else:
                    for i in range(PARTS):
                        back_copy(i, p, p).wait_recv()
            here = pl.ds(pl.multiple_of(128 * b, 128), 128)
            pieces = [(b * per + k, i) for k in range(per) for i in range(PARTS)]
            first_part = jnp.concatenate([back[p, i, 0:own] for p, i in pieces], axis=0).T
            rest = []
            for p, i in pieces:
                piece = back[p, i, own : own + half]
                rest += [piece, pltpu.roll(piece, 64, 1)]
            second_part = jnp.concatenate(rest, axis=0).T
            for f in range(3):
                out[0, f, :, here] = state[0, f, :, here] - first_part[32 * f : 32 * f + 32]
            out[1, 0, :, here] = state[1, 0, :, here] - first_part[96:128]
            for f in (1, 2):
                out[1, f, :, here] = state[1, f, :, here] - second_part[32 * f - 32 : 32 * f]

    def back_sent(k, carry):
        p = lax.rem(me + k, ntm)
        for i in range(PARTS):
            back_copy(i, p, me).wait_send()
        return carry

    lax.fori_loop(1, ntm, back_sent, 0)


def solution(mesh):
    ntm, nsp = mesh.shape["tm"], mesh.shape["space"]

    def on_device(state, initial):
        cols = state.shape[3]
        width = cols // ntm
        vmem = pltpu.VMEM
        updated = pl.pallas_call(
            functools.partial(kernel, ntm, nsp),
            out_shape=vmem(state.shape, f32),
            in_specs=[pl.BlockSpec(memory_space=pl.ANY)] * 3,
            out_specs=pl.BlockSpec(memory_space=vmem),
            scratch_shapes=[
                vmem(state.shape, f32),
                vmem((256, 256), jnp.bfloat16),
                vmem((2, 3, 8, cols), f32),
                vmem((3, 32, cols), f32),
                vmem((3, 8, cols), f32),
                vmem((128, cols), f32),
                vmem((2, ntm, width + 16, 128), f32),
                vmem((2 * ntm, width + 16, 128), f32),
                vmem((2 * ntm, width // PARTS + 8, 128), f32),
                vmem((ntm, PARTS, 3 * width // (2 * PARTS), 128), f32),
                vmem((ntm, PARTS, 3 * width // (2 * PARTS), 128), f32),
                pltpu.SemaphoreType.DMA((7,)),
                pltpu.SemaphoreType.DMA((7,)),
                pltpu.SemaphoreType.DMA((2, PARTS, ntm)),
                pltpu.SemaphoreType.DMA((2, PARTS, ntm)),
                pltpu.SemaphoreType.DMA((PARTS, ntm)),
                pltpu.SemaphoreType.DMA((PARTS, ntm)),
                pltpu.SemaphoreType.DMA((3,)),
                pltpu.SMEM((ntm,), f32),
            ],
            compiler_params=pltpu.CompilerParams(
                collective_id=0, has_side_effects=True, vmem_limit_bytes=60 << 20
            ),
        )(state, initial, stencil_table())
        return updated

    return jax.shard_map(
        on_device,
        mesh=mesh,
        in_specs=(P("tm", None, "space", None), P(None, "space", None)),
        out_specs=P("tm", None, "space", None),
        check_vma=False,
    )
```

```python
import functools
import math

import jax
import jax.numpy as jnp
import numpy as np
from jax import lax
from jax.experimental import pallas as pl
from jax.experimental.pallas import tpu as pltpu
from jax.sharding import PartitionSpec as P

SWEEPS = 4
ALPHA = 0.1
A = 1.0 / 1.8
CHUNK = 64
PARTS = 1
R = 40
MESH = pl.DeviceIdType.MESH
f32 = jnp.float32


def sweep_weights():
    return [
        1.0 / (1.15 - 0.85 * math.cos(math.pi * (2 * m + 1) / (2 * SWEEPS))) for m in range(SWEEPS)
    ]


def stencil_table():
    table = np.zeros((2, 128, 128), np.float32)
    for f in range(3):
        for r in range(R):
            here = f * R + r
            for step in (-1, 1):
                if 0 <= r + step < R:
                    table[0, here + step, here] = 4.0
                    if f != 1:
                        table[0, (2 - f) * R + r + step, here] = -5.0 * step
    for r in range(R):
        table[0, 2 * R + r, R + r] = 6.0
        table[0, R + r, 2 * R + r] = -6.0
        table[1, R + r, r] = table[1, r, R + r] = -5.0
    one = np.concatenate(list(table), axis=1)
    return jnp.asarray(0.25 * np.concatenate([one, one], axis=0), jnp.bfloat16)


def far_first(shape):
    span = [[(d, min(d, n - d)) for d in range(n)] for n in shape]
    every = [(x, z, c) for x in span[0] for z in span[1] for c in span[2]]
    every.sort(key=lambda d: -(d[0][1] + d[1][1]))
    return [tuple(a[0] for a in d) for d in every if any(a[0] for a in d)]


def residual_tile(load, j, before):
    sub = lax.broadcasted_iota(jnp.int32, (8, 1), 0)

    def near(f):
        here, after, ahead = load(f, j), load(f, (j + 1) % 5), load(f, (j + 4) % 5)
        cols = here.shape[1]
        north = pltpu.roll(jnp.where(sub == 0, after, here), 7, 0)
        south = pltpu.roll(jnp.where(sub == 7, ahead, here), 1, 0)
        east = pltpu.roll(here, cols - 1, 1)
        west = pltpu.roll(here, 1, 1)
        return here, east, west, north, south

    e, ee, ew, en, es = near(0)
    u, ue, uw, un, us = near(1)
    v, ve, vw, vn, vs = near(2)
    mass = 0.25 * (
        ((1.0 + ee) * ue - (1.0 + ew) * uw) + ((1.0 + en) * vn - (1.0 + es) * vs)
    ) - 0.2 * (ee + ew + en + es - 4.0 * e)
    east = (
        0.25 * (u * (ue - uw) + v * (un - us) + (ee - ew))
        - 0.3 * v
        - 0.2 * (ue + uw + un + us - 4.0 * u)
    )
    north = (
        0.25 * (u * (ve - vw) + v * (vn - vs) + (en - es))
        + 0.3 * u
        - 0.2 * (ve + vw + vn + vs - 4.0 * v)
    )
    return [x - before(f, j) + t for f, (x, t) in enumerate(((e, mass), (u, east), (v, north)))]


def kernel(
    ntm,
    nsp,
    state_hbm,
    initial,
    stencil_hbm,
    out,
    state,
    stencil,
    halo,
    prev,
    prev_halo,
    res,
    send,
    s_buf,
    y_buf,
    corr,
    back,
    ex_send,
    ex_recv,
    in_send,
    in_recv,
    back_send,
    back_recv,
    load_sem,
    fade,
):
    me = lax.axis_index("tm")
    sp = lax.axis_index("space")
    nxt, prv = lax.rem(me + 1, ntm), lax.rem(me + ntm - 1, ntm)
    up, dn = lax.rem(sp + 1, nsp), lax.rem(sp + nsp - 1, nsp)
    cols = state.shape[3]
    shape = (4, ntm // 8, 2)
    x, z, c = lax.div(me, 2 * shape[1]), lax.rem(lax.div(me, 2), shape[1]), lax.rem(me, 2)
    others = [
        (lax.rem(x + dx, shape[0]) * shape[1] + lax.rem(z + dz, shape[1])) * 2 + lax.rem(c + dc, 2)
        for dx, dz, dc in far_first(shape)
    ]
    steps = 2 * ntm
    width = cols // ntm
    sub8 = lax.broadcasted_iota(jnp.int32, (8, 1), 0)

    barrier = pltpu.get_barrier_semaphore()
    around = [(me, up), (me, dn), (nxt, up), (nxt, dn), (prv, up), (prv, dn)]
    for other in around:
        pl.semaphore_signal(barrier, inc=1, device_id=other, device_id_type=MESH)

    for p in others:
        pl.semaphore_signal(barrier, inc=1, device_id=(p, sp), device_id_type=MESH)
    loads = [
        pltpu.make_async_copy(state_hbm.at[t], state.at[t], load_sem.at[t]) for t in (1, 0)
    ] + [pltpu.make_async_copy(stencil_hbm, stencil, load_sem.at[2])]
    for copy in loads:
        copy.start()

    def clear(n, carry):
        s_buf[n, 0:5, :] = jnp.zeros((5, 128), f32)
        s_buf[n, 11 + width : 16 + width, :] = jnp.zeros((5, 128), f32)
        return carry

    lax.fori_loop(0, steps, clear, 0, unroll=8)
    pl.semaphore_wait(barrier, ntm - 1 + len(around))

    def exchange(i, src, dst, device):
        return pltpu.make_async_remote_copy(
            src_ref=src,
            dst_ref=dst,
            send_sem=ex_send.at[i],
            recv_sem=ex_recv.at[i],
            device_id=device,
            device_id_type=MESH,
        )

    low, high = pl.ds(0, 4), pl.ds(4, 4)
    rows_hi = pl.ds(28, 4)

    def edges():
        return [
            exchange(0, state_hbm.at[:, :, low], halo.at[:, :, low], (me, dn)),
            exchange(1, state_hbm.at[:, :, rows_hi], halo.at[:, :, high], (me, up)),
        ]

    def handed(last):
        return [
            exchange(4, last, prev, (nxt, sp)),
            exchange(5, last.at[:, low], prev_halo.at[:, low], (nxt, dn)),
            exchange(6, last.at[:, rows_hi], prev_halo.at[:, high], (nxt, up)),
        ]

    normal = edges() + handed(state_hbm.at[1])
    for copy in normal[:2]:
        copy.start()

    @pl.when(me != ntm - 1)
    def _():
        for copy in normal[2:]:
            copy.start()

    @pl.when(me == ntm - 1)
    def _():
        for copy in handed(initial):
            copy.start()

    own = width // PARTS

    def in_copy(t, i, p, slot):
        start = 5 if i == 0 else 12 + own * i
        end = 11 + width if t == 1 or i == PARTS - 1 else 12 + own * (i + 1)
        rows = pl.ds(start, end - start)
        return pltpu.make_async_remote_copy(
            src_ref=send.at[t, p, rows],
            dst_ref=s_buf.at[slot, rows],
            send_sem=in_send.at[t, i, p],
            recv_sem=in_recv.at[t, i, lax.div(slot, 2)],
            device_id=(p, sp),
            device_id_type=MESH,
        )

    res[3 * R :, :] = jnp.zeros((res.shape[0] - 3 * R, cols), f32)

    def step_out(t):
        def load(f, j):
            return state[t, f, 8 * j : 8 * j + 8, :] if j < 4 else halo[t, f]

        def before(f, j):
            if t == 1:
                return state[0, f, 8 * j : 8 * j + 8, :] if j < 4 else halo[0, f]
            return prev[f, 8 * j : 8 * j + 8, :] if j < 4 else prev_halo[f]

        last = residual_tile(load, 4, before)
        held = last
        for j in range(4):
            now = residual_tile(load, j, before)
            for f in range(3):
                res[f * R + 8 * j : f * R + 8 * j + 8, :] = pltpu.roll(
                    jnp.where(sub8 < 4, now[f], held[f]), 4, 0
                )
            held = now
        for f in range(3):
            res[f * R + 32 : f * R + 40, :] = pltpu.roll(
                jnp.where(sub8 < 4, last[f], held[f]), 4, 0
            )
        for b in range(cols // 128):
            block = res[:, 128 * b : 128 * b + 128].T
            for i in range(128 // width):
                p = b * (128 // width) + i
                mine = block[width * i : width * i + width]
                send[t, p, 8 : 8 + width, :] = mine
                send[t, (p + 1) % ntm, 4:8, :] = mine[width - 4 :]
                send[t, (p - 1) % ntm, 8 + width : 12 + width, :] = mine[:4]

    def go(t, i):
        for p in others:
            in_copy(t, i, p, 2 * me + t).start()

    gain = jnp.float32(1.0)
    for n in range(ntm):
        fade[n] = gain
        gain = gain * (A * A)
    for copy in loads:
        copy.wait()
    for copy in normal[:2]:
        copy.wait_recv()
    step_out(1)
    go(1, 0)
    for copy in normal[2:]:
        copy.wait_recv()
    step_out(0)
    go(0, 0)
    for i in range(1, PARTS):
        for p in others:
            in_copy(0, i - 1, p, 2 * me).wait_send()
            in_copy(0, i, p, 2 * me).start()
    for t in range(2):
        s_buf[2 * me + t, 5 : 11 + width, :] = send[t, me, 5 : 11 + width, :]

    def landed(i):
        def one(k, carry):
            p = lax.rem(me + k, ntm)
            if i == 0:
                in_copy(1, 0, p, 2 * p + 1).wait_recv()
            in_copy(0, i, p, 2 * p).wait_recv()
            return carry

        lax.fori_loop(1, ntm, one, 0)

    rows = own + 8
    weights = sweep_weights()
    closing = ALPHA / (1.0 - ALPHA * A**steps)
    zero = jnp.zeros((rows, 128), f32)

    def solve(i):
        start = 8 + own * i

        def rhs(n):
            after = s_buf[n, start + own : start + own + 8, :]
            ahead = s_buf[n, start - 8 : start, :]
            return jnp.concatenate(
                [s_buf[n, start : start + own, :], jnp.where(sub8 < 4, after, ahead)], axis=0
            )

        def first(k, h):
            for q in range(CHUNK):
                n = CHUNK * k + q
                h = A * (rhs(n) + h)
                y_buf[n] = (0.2 * weights[0]) * h
            return h

        h = lax.fori_loop(0, steps // CHUNK, first, zero)
        wrap = (0.2 * A * weights[0] * closing) * h
        for m in range(1, SWEEPS):
            keep, gain = 1.0 - weights[m], 0.2 * weights[m]
            kept = rows
            if m == SWEEPS - 1:
                keep, gain, kept = 5.0 * keep, 5.0 * gain, own

            def sweep(k, carry, keep=keep, gain=gain, kept=kept):
                h, wrap = carry
                ys = []
                for q in range(CHUNK):
                    ys.append(y_buf[CHUNK * k + q] + wrap)
                    wrap = A * wrap
                y = jnp.concatenate(ys, axis=0)
                high_part = y.astype(jnp.bfloat16)
                low_part = (y - high_part.astype(f32)).astype(jnp.bfloat16)
                both = jnp.concatenate([high_part, low_part], axis=1)
                mixed = jnp.dot(both, stencil[...], preferred_element_type=f32)
                for q in range(CHUNK):
                    n = CHUNK * k + q
                    part = mixed[rows * q : rows * q + rows]
                    here, cross, even = part[:, :128], part[:, 128:], ys[q]
                    beside = pltpu.roll(even + cross, rows - 1, 0) + pltpu.roll(even - cross, 1, 0)
                    s = rhs(n) if kept == rows else s_buf[n, start : start + own, :]
                    h = A * (((s + here[:kept]) + beside[:kept]) + h)
                    y_buf[n, 0:kept, :] = keep * ys[q][:kept] + gain * h
                return h, wrap

            h, _ = lax.fori_loop(0, steps // CHUNK, sweep, (zero[:kept], wrap))
            wrap = (gain * A * closing) * h
        return wrap

    def back_copy(i, d, slot):
        return pltpu.make_async_remote_copy(
            src_ref=corr.at[d, i],
            dst_ref=back.at[slot, i],
            send_sem=back_send.at[i, d],
            recv_sem=back_recv.at[i, slot],
            device_id=(d, sp),
            device_id_type=MESH,
        )

    lane = lax.broadcasted_iota(jnp.int32, (own, 128), 1)
    below = [lane < 32, lane < 64, lane < 96]
    half = own // 2

    def finish(i, d, wrap):
        closed = wrap * fade[d]
        one = y_buf[2 * d, 0:own, :] + closed
        two = y_buf[2 * d + 1, 0:own, :] + A * closed
        moved = [pltpu.roll(one, 124 - 8 * f, 1) for f in range(3)]
        corr[d, i, 0:own, :] = jnp.where(
            below[0],
            moved[0],
            jnp.where(below[1], moved[1], jnp.where(below[2], moved[2], pltpu.roll(two, 92, 1))),
        )
        top, end = two[0:half], two[half:own]
        corr[d, i, own : own + half, :] = jnp.where(
            below[0][0:half],
            pltpu.roll(top, 84, 1),
            jnp.where(
                below[1][0:half],
                pltpu.roll(top, 76, 1),
                jnp.where(below[2][0:half], pltpu.roll(end, 20, 1), pltpu.roll(end, 12, 1)),
            ),
        )

    for i in range(PARTS):
        landed(i)
        wrap = solve(i)
        for k, d in enumerate(others):
            finish(i, d, wrap)
            if k > 0:
                back_copy(i, others[k - 1], me).start()
        finish(i, me, wrap)
        back_copy(i, others[-1], me).start()
    back[me] = corr[me]

    for copy in normal:
        copy.wait_send()

    def in_sent(k, carry):
        p = lax.rem(me + k, ntm)
        in_copy(1, 0, p, 2 * p + 1).wait_send()
        in_copy(0, PARTS - 1, p, 2 * p).wait_send()
        return carry

    lax.fori_loop(1, ntm, in_sent, 0)

    per = 128 // width
    pairs = shape[1] * 2 // per
    pair = lax.div(z * 2, per)
    for dx in sorted(range(shape[0]), key=lambda d: -min(d, shape[0] - d)):
        for dz in range(pairs - 1, -1, -1):
            b = lax.rem(x + dx, shape[0]) * pairs + lax.rem(pair + dz, pairs)
            for k in range(per):
                p = b * per + k
                if dx == 0 and dz == 0:

                    @pl.when(p != me)
                    def _():
                        for i in range(PARTS):
                            back_copy(i, p, p).wait_recv()

                else:
                    for i in range(PARTS):
                        back_copy(i, p, p).wait_recv()
            here = pl.ds(pl.multiple_of(128 * b, 128), 128)
            pieces = [(b * per + k, i) for k in range(per) for i in range(PARTS)]
            first_part = jnp.concatenate([back[p, i, 0:own] for p, i in pieces], axis=0).T
            rest = []
            for p, i in pieces:
                piece = back[p, i, own : own + half]
                rest += [piece, pltpu.roll(piece, 64, 1)]
            second_part = jnp.concatenate(rest, axis=0).T
            for f in range(3):
                out[0, f, :, here] = state[0, f, :, here] - first_part[32 * f : 32 * f + 32]
            out[1, 0, :, here] = state[1, 0, :, here] - first_part[96:128]
            for f in (1, 2):
                out[1, f, :, here] = state[1, f, :, here] - second_part[32 * f - 32 : 32 * f]

    def back_sent(k, carry):
        p = lax.rem(me + k, ntm)
        for i in range(PARTS):
            back_copy(i, p, me).wait_send()
        return carry

    lax.fori_loop(1, ntm, back_sent, 0)


def solution(mesh):
    ntm, nsp = mesh.shape["tm"], mesh.shape["space"]

    def on_device(state, initial):
        cols = state.shape[3]
        width = cols // ntm
        vmem = pltpu.VMEM
        updated = pl.pallas_call(
            functools.partial(kernel, ntm, nsp),
            out_shape=vmem(state.shape, f32),
            in_specs=[pl.BlockSpec(memory_space=pl.ANY)] * 3,
            out_specs=pl.BlockSpec(memory_space=vmem),
            scratch_shapes=[
                vmem(state.shape, f32),
                vmem((256, 256), jnp.bfloat16),
                vmem((2, 3, 8, cols), f32),
                vmem((3, 32, cols), f32),
                vmem((3, 8, cols), f32),
                vmem((128, cols), f32),
                vmem((2, ntm, width + 16, 128), f32),
                vmem((2 * ntm, width + 16, 128), f32),
                vmem((2 * ntm, width // PARTS + 8, 128), f32),
                vmem((ntm, PARTS, 3 * width // (2 * PARTS), 128), f32),
                vmem((ntm, PARTS, 3 * width // (2 * PARTS), 128), f32),
                pltpu.SemaphoreType.DMA((7,)),
                pltpu.SemaphoreType.DMA((7,)),
                pltpu.SemaphoreType.DMA((2, PARTS, ntm)),
                pltpu.SemaphoreType.DMA((2, PARTS, ntm)),
                pltpu.SemaphoreType.DMA((PARTS, ntm)),
                pltpu.SemaphoreType.DMA((PARTS, ntm)),
                pltpu.SemaphoreType.DMA((3,)),
                pltpu.SMEM((ntm,), f32),
            ],
            compiler_params=pltpu.CompilerParams(
                collective_id=0, has_side_effects=True, vmem_limit_bytes=60 << 20
            ),
        )(state, initial, stencil_table())
        return updated

    return jax.shard_map(
        on_device,
        mesh=mesh,
        in_specs=(P("tm", None, "space", None), P(None, "space", None)),
        out_specs=P("tm", None, "space", None),
        check_vma=False,
    )
```
